512 devices in a mesh: dp: 32 (over y, x), seq: 16 (over z, core).
Axes of the slice: x: 4, y: 8, z: 8, core: 2. Of those that a mesh axis runs over, the one named last changes fastest.
Arguments:
- queries: bfloat16 [32, 2048, 3072], P('dp', 'seq'), may hold values from -6 to 6
- key_states: bfloat16 [32, 2048, 3072], P('dp', 'seq'), may hold values from -6 to 6
- value_states: bfloat16 [32, 2048, 3072], P('dp', 'seq'), may hold values from -6 to 6
- cotangent: bfloat16 [32, 2048, 128], P('dp', 'seq'), may hold values from -6 to 6
- norm_gains: float32 [2, 128], P(None, 'dp'), may hold values from 0.5 to 1.5
- tile_lists: int32 [32, 4], replicated, may hold values from -1 to 31, as said below
- clip_lengths: int32 [32], P('dp'), may hold values from 1024 to 2048
Outputs:
- query_grad: bfloat16 [32, 2048, 3072], P('dp', 'seq')
- key_grad: bfloat16 [32, 2048, 3072], P('dp', 'seq')
- value_grad: bfloat16 [32, 2048, 3072], P('dp', 'seq')
- gain_grad: float32 [2, 128], P(None, 'dp')
The draws below stay inside these ranges and needn't reach their ends.
Inputs may be any that keep to these rules, and one draw needn't show every extreme that they name: `tile_lists`: row i names tile 0 in its first slot; for i > 0 its second slot names tile i; the other names of a row are distinct tiles other than 0; between 3 and 4 slots of a row name tiles and the rest are -1; row 0 has at least one -1.
All inputs are finite; a program needn't handle non-finite values.
Results may differ from the reference program's by a relative error of at most 0.0086.
Values may be sent and summed in bfloat16 or wider, within the bound.
A program may use at most 128 MiB of HBM per device.

```python
import math
import jax
import jax.numpy as jnp
from jax import lax

HEADS = 24
HEAD_DIM = 128
TILE = 64
NB = 4
CLIPS = 32
NTOK = 2048
NTILES = 32
HALF = 2


def draw_tile_lists(key, part):
    first_key, second_key = jax.random.split(key)
    row_ids = jnp.arange(NTILES, dtype=jnp.int32)
    noise = jax.random.randint(first_key, (NTILES, NTILES), 0, 64, dtype=jnp.int32)
    spread = jnp.abs(row_ids[:, None] - row_ids[None, :])
    nearness = jnp.maximum(8 - spread, 0) * 4
    ranking = (nearness + noise) * NTILES + row_ids[None, :]
    ranking = jnp.where(spread == 0, jnp.int32(1 << 30), ranking)
    ranking = jnp.where(row_ids[None, :] == 0, -1, ranking)
    chosen = lax.top_k(ranking, NB - 1)[1].astype(jnp.int32)
    counts = jax.random.randint(second_key, (NTILES, 1), NB // 2, NB, dtype=jnp.int32)
    counts = jnp.where(row_ids[:, None] == 0, NB // 2, counts)
    slots = jnp.arange(NB - 1, dtype=jnp.int32)
    chosen = jnp.where(slots[None, :] < counts, chosen, -1)
    return jnp.concatenate([jnp.zeros((NTILES, 1), jnp.int32), chosen], axis=1)


def plant(drawn, key, low, top_value):
    extent = drawn.shape
    place = [jax.random.randint(jax.random.fold_in(key, axis), (), 0, extent[axis]) for axis in range(len(extent))]
    drawn = drawn.at[tuple(place)].set(low)
    longest = extent.index(max(extent))
    place[longest] = (place[longest] + 1) % extent[longest]
    return drawn.at[tuple(place)].set(top_value)


def shard_levels(stream_key, shape, cuts, low, high):
    def one(dim, shards_of):
        heights = jax.random.uniform(jax.random.fold_in(jax.random.fold_in(stream_key, 6), dim), (shards_of,), jnp.float32, low / len(cuts), high / len(cuts))
        return jnp.repeat(jnp.exp(heights), shape[dim] // shards_of).reshape((-1,) + (1,) * (len(shape) - dim - 1))

    level = one(*cuts[0])
    for cut in cuts[1:]:
        level = level * one(*cut)
    return level


def gaussian(own_key, extent, width, limit, pieces=(), kind=jnp.bfloat16):
    factor_of = shard_levels(own_key, extent, pieces, -0.22, 0.18) if pieces else 1.0
    array = jax.random.normal(own_key, extent, jnp.float32) * width * factor_of
    return jnp.minimum(jnp.maximum(array, -limit), limit).astype(kind)


def setup_inputs(seed: int = 0) -> dict:
    keys = jax.random.split(jax.random.key(seed), 8)
    return {
        "queries": gaussian(keys[0], (CLIPS, NTOK, HEADS * HEAD_DIM), 1.0, 6.0, ((0, 32), (1, 16))),
        "key_states": gaussian(keys[1], (CLIPS, NTOK, HEADS * HEAD_DIM), 1.0, 6.0, ((0, 32), (1, 16))),
        "value_states": gaussian(keys[2], (CLIPS, NTOK, HEADS * HEAD_DIM), 1.0, 6.0, ((0, 32), (1, 16))),
        "cotangent": gaussian(keys[3], (CLIPS, NTOK, HEAD_DIM), 1.0, 6.0, ((0, 32), (1, 16))),
        "norm_gains": jnp.clip(1.0 + 0.1 * jax.random.normal(keys[4], (2, HEAD_DIM), jnp.float32), 0.5, 1.5),
        "tile_lists": draw_tile_lists(jax.random.fold_in(keys[7], 71), 0),
        "clip_lengths": plant(jax.random.randint(keys[6], (CLIPS,), NTOK // 2, NTOK + 1), jax.random.fold_in(keys[6], 1), NTOK // 2, NTOK).astype(jnp.int32),
    }


EPS = 1e-06

def rms_parts(raw_rows, gain_row):
    widened = raw_rows.astype(jnp.float32).reshape(raw_rows.shape[0], HEADS, HEAD_DIM)
    inverse = lax.rsqrt(lax.optimization_barrier(jnp.mean(widened * widened, axis=-1, keepdims=True)) + EPS)
    return (widened, inverse, (widened * inverse * gain_row).astype(jnp.bfloat16))

def rms_back(widened, inverse, gain_row, upstream):
    incoming = upstream.astype(jnp.float32)
    scaled = incoming * gain_row
    inner_sum = lax.optimization_barrier(jnp.mean(widened * scaled, axis=-1, keepdims=True))
    grad_rows = inverse * scaled - widened * inverse * inverse * inverse * inner_sum
    return (grad_rows, lax.optimization_barrier(jnp.sum(incoming * widened * inverse, axis=(0, 1))))

def block_grads(query_tiles, cot_tiles, list_block, key_tiles, value_tiles, length):
    factor = 1.0 / math.sqrt(HEAD_DIM)
    safe_ids = jnp.maximum(list_block, 0)
    key_rows = key_tiles[safe_ids].astype(jnp.float32)
    value_rows = value_tiles[safe_ids].astype(jnp.float32)
    positions = safe_ids[:, :, None] * TILE + jnp.arange(TILE, dtype=jnp.int32)[None, None, :]
    usable = jnp.logical_and(list_block[:, :, None] >= 0, positions < length).astype(jnp.float32)
    query_wide = query_tiles.astype(jnp.float32)
    cot_wide = cot_tiles.astype(jnp.float32)
    scores = jnp.einsum('gqhd,gnkhd->ghqnk', query_wide, key_rows) * factor
    weights = jnp.exp(scores) * usable[:, None, None, :, :]
    prob_rows = weights / lax.optimization_barrier(jnp.sum(weights, axis=(3, 4), keepdims=True))
    prob_low = lax.optimization_barrier(prob_rows.astype(jnp.bfloat16)).astype(jnp.float32)
    attended = jnp.einsum('ghqnk,gnkhd->gqhd', prob_low, value_rows)
    diag_term = lax.optimization_barrier(jnp.sum(cot_wide[:, :, None, :] * attended, axis=-1))
    grad_probs = jnp.einsum('gqd,gnkhd->ghqnk', cot_wide, value_rows)
    grad_scores = prob_rows * (grad_probs - jnp.transpose(diag_term, (0, 2, 1))[:, :, :, None, None])
    grad_low = lax.optimization_barrier(grad_scores.astype(jnp.bfloat16)).astype(jnp.float32)
    grad_query = (jnp.einsum('ghqnk,gnkhd->gqhd', grad_low, key_rows) * factor).astype(jnp.bfloat16)
    grad_keys = jnp.einsum('ghqnk,gqhd->gnkhd', grad_low, query_wide) * factor
    grad_values = jnp.einsum('ghqnk,gqd->gnkhd', prob_low, cot_wide)
    return (safe_ids, grad_query, grad_keys, grad_values)

def merge_parts(accum):
    parts = accum.reshape(HALF, NTILES, TILE, HEADS, HEAD_DIM)
    rounded = lax.optimization_barrier(parts.astype(jnp.bfloat16)).astype(jnp.float32)
    return lax.optimization_barrier(jnp.sum(rounded, axis=0)).astype(jnp.bfloat16)

def one_clip(packed, norm_gains, tile_lists):
    query_rows, key_input, value_input, cot_rows, length = packed
    query_wide, query_inv, query_norm = rms_parts(query_rows, norm_gains[0])
    keys_wide, keys_inv, keys_norm = rms_parts(key_input, norm_gains[1])
    positions = jnp.arange(NTOK, dtype=jnp.int32)
    cot_live = jnp.where((positions < length)[:, None], cot_rows, jnp.zeros_like(cot_rows))
    block_size = math.gcd(NTILES, 8)
    block_count = NTILES // block_size
    key_tiles = keys_norm.reshape(NTILES, TILE, HEADS, HEAD_DIM)
    value_tiles = value_input.reshape(NTILES, TILE, HEADS, HEAD_DIM)
    class_offset = (jnp.arange(block_size, dtype=jnp.int32) % HALF * NTILES)[:, None]

    def tile_step(carried, inputs):
        acc_keys, acc_values = carried
        query_block, cot_block, list_block = inputs
        safe_ids, grad_query, grad_keys, grad_values = block_grads(query_block, cot_block, list_block, key_tiles, value_tiles, length)
        where_rows = (safe_ids + class_offset).reshape(-1)
        acc_keys = acc_keys.at[where_rows].add(grad_keys.reshape(-1, TILE, HEADS, HEAD_DIM))
        acc_values = acc_values.at[where_rows].add(grad_values.reshape(-1, TILE, HEADS, HEAD_DIM))
        return ((acc_keys, acc_values), grad_query)
    empty_acc = jnp.zeros((HALF * NTILES, TILE, HEADS, HEAD_DIM), jnp.float32)
    scanned = (query_norm.reshape(block_count, block_size, TILE, HEADS, HEAD_DIM), cot_live.reshape(block_count, block_size, TILE, HEAD_DIM), tile_lists.reshape(block_count, block_size, NB))
    (acc_keys, acc_values), grad_query = lax.scan(tile_step, (empty_acc, empty_acc), scanned)
    query_grad_norm = grad_query.reshape(NTOK, HEADS, HEAD_DIM)
    key_grad_norm = merge_parts(acc_keys).reshape(NTOK, HEADS, HEAD_DIM)
    value_grad = merge_parts(acc_values).reshape(NTOK, HEADS * HEAD_DIM)
    query_grad, gain_query = rms_back(query_wide, query_inv, norm_gains[0], query_grad_norm)
    key_grad, gain_keys = rms_back(keys_wide, keys_inv, norm_gains[1], key_grad_norm)
    return (query_grad.astype(jnp.bfloat16).reshape(NTOK, HEADS * HEAD_DIM), key_grad.astype(jnp.bfloat16).reshape(NTOK, HEADS * HEAD_DIM), value_grad, jnp.stack([gain_query, gain_keys], 0))

def reference(queries, key_states, value_states, cotangent, norm_gains, tile_lists, clip_lengths):

    def clip_step(packed):
        return one_clip(packed, norm_gains, tile_lists)
    query_grad, key_grad, value_grad, gain_terms = lax.map(clip_step, (queries, key_states, value_states, cotangent, clip_lengths))
    factor = 1.0 / math.sqrt(CLIPS * NTOK * HEADS)
    return (query_grad, key_grad, value_grad, lax.optimization_barrier(jnp.sum(gain_terms, axis=0)) * factor)
```

```python
import functools
import math


import jax
import jax.numpy as jnp
from jax import lax
from jax.experimental import pallas as pl
from jax.experimental.pallas import tpu as pltpu
import ml_dtypes
from jax.sharding import PartitionSpec as P

HEAD_DIM = 128
TILE = 64
EPS = 1e-06
BLOCK = 256
COLS = 4
ROWS = 8
MESH = pl.DeviceIdType.MESH
FACTOR = 1.0 / math.sqrt(HEAD_DIM)
BLOCKED = -30000.0
TWICE = math.log(2.0) / FACTOR
COMPUTE = True


def wait_bytes(ref, sem):
    pltpu.make_async_copy(ref, ref, sem).wait()


def rms_inverse(wide):
    return lax.rsqrt(jnp.mean(wide * wide, axis=-1, keepdims=True) + EPS)


def rms_back(wide, inverse, gain_row, upstream):
    scaled = upstream * gain_row
    inner = jnp.mean(wide * scaled, axis=-1, keepdims=True)
    grad = inverse * scaled - wide * (inverse * inverse * inverse * inner)
    return grad.astype(jnp.bfloat16), jnp.sum(upstream * wide * inverse, axis=0, keepdims=True)


def kernel(
    sizes,
    q_in, k_in, v_in, c_in, g_in, info,
    dq_out, dk_out, dv_out, gain_out,
    xq, xk, xv, cot, oq, ok, ov,
    qa, ka, kt, live, wbuf, gbuf, dk_acc, dv_acc,
    gx, gy, ysrc, gains, gacc, hz, hx, hy, hsrc, hsrc2,
    fsend, frecv, csend, crecv, rsend, orecv, gsend, grecv,
):
    chips, shard, per_chip = sizes
    seq = lax.axis_index("seq")
    dp = lax.axis_index("dp")
    chip, core = seq // 2, seq % 2
    row, col = dp // COLS, dp % COLS
    total = 2 * chips * shard
    blocks = total // BLOCK

    barrier = pltpu.get_barrier_semaphore()

    def greet_seq(i, carry):
        pl.semaphore_signal(barrier, inc=1, device_id={"seq": (seq + i) % (2 * chips)}, device_id_type=MESH)
        return carry

    def greet_col(i, carry):
        pl.semaphore_signal(barrier, inc=1, device_id={"dp": row * COLS + (col + i) % COLS}, device_id_type=MESH)
        return carry

    def greet_row(i, carry):
        pl.semaphore_signal(barrier, inc=1, device_id={"dp": (row + i) % ROWS * COLS + col}, device_id_type=MESH)
        return carry

    lax.fori_loop(1, 2 * chips, greet_seq, 0)
    lax.fori_loop(1, COLS, greet_col, 0)
    lax.fori_loop(1, ROWS, greet_row, 0)
    pl.semaphore_wait(barrier, 2 * chips - 1 + COLS - 1 + ROWS - 1)

    arrays = ((q_in, xq), (k_in, xk), (v_in, xv))
    my_rows = pl.ds(pl.multiple_of(seq * shard, shard), shard)

    def send_gx(i, carry):
        pltpu.make_async_remote_copy(
            src_ref=g_in, dst_ref=gx.at[col], send_sem=gsend.at[0], recv_sem=grecv.at[0],
            device_id={"dp": row * COLS + (col + i) % COLS}, device_id_type=MESH,
        ).start()
        return carry

    lax.fori_loop(1, COLS, send_gx, 0)
    gx[col] = g_in[...]

    def far(i):
        half = (i + 1) // 2
        return (chip + chips // 2 + half * (1 - 2 * (i % 2))) % chips

    def send_cot(i, carry):
        pltpu.make_async_remote_copy(
            src_ref=c_in.at[0], dst_ref=cot.at[chip, core], send_sem=csend.at[0], recv_sem=crecv.at[0],
            device_id={"seq": 2 * far(i) + core}, device_id_type=MESH,
        ).start()
        return carry

    lax.fori_loop(0, chips - 1, send_cot, 0)
    pltpu.make_async_copy(c_in.at[0], cot.at[chip, core], crecv.at[0]).start()

    def spread_head(which):
        owner, slot = which % 2, which // 2

        def to_chip(target, start_kind):
            lanes = pl.ds(pl.multiple_of((target * per_chip + which) * HEAD_DIM, HEAD_DIM), HEAD_DIM)
            for index, (source, landing) in enumerate(arrays):
                src = source.at[0, :, lanes]
                dst = landing.at[slot, my_rows, :]
                if start_kind == "local":
                    pltpu.make_async_copy(src, dst, frecv.at[slot, index]).start()
                else:
                    pltpu.make_async_remote_copy(
                        src_ref=src, dst_ref=dst, send_sem=fsend.at[index], recv_sem=frecv.at[slot, index],
                        device_id={"seq": 2 * target + owner}, device_id_type=MESH,
                    ).start()

        def remote(i, carry):
            to_chip(far(i), "remote")
            return carry

        lax.fori_loop(0, chips - 1, remote, 0)

        @pl.when(core == owner)
        def _():
            to_chip(chip, "local")

        @pl.when(core != owner)
        def _():
            to_chip(chip, "remote")

    for which in range(per_chip):
        spread_head(which)

    wait_bytes(gx.at[pl.ds(0, COLS - 1)], grecv.at[0])
    ysrc[...] = gx[0] + gx[1] + gx[2] + gx[3]

    lanes = lax.broadcasted_iota(jnp.int32, (TILE, HEAD_DIM), 1)
    rows64 = lax.broadcasted_iota(jnp.int32, (TILE, HEAD_DIM), 0)
    length = info[4:5, :]
    high = float(ml_dtypes.bfloat16(TWICE))
    low = float(ml_dtypes.bfloat16(TWICE - high))

    def mask_tile(j, carry):
        count = jnp.zeros((1, HEAD_DIM), jnp.int32)
        for n in range(4):
            count = count + (info[n : n + 1, :] == j).astype(jnp.int32)
        count = jnp.broadcast_to(count, (TILE, HEAD_DIM))
        usable = jnp.logical_and(count > 0, j * TILE + rows64 < length)
        first = jnp.where(usable, jnp.where(count > 1, high, 0.0), BLOCKED)
        second = jnp.where(count > 1, low, 0.0)
        bias = jnp.where(lanes < 32, first, jnp.where(lanes < 64, second, 0.0))
        here = pl.ds(pl.multiple_of(j * TILE, TILE), TILE)
        ka[here, HEAD_DIM:] = bias.astype(jnp.bfloat16)
        mark = jnp.logical_and(lanes % 32 == j, lanes < 64)
        qa[here, HEAD_DIM:] = jnp.where(mark, 1.0, 0.0).astype(jnp.bfloat16)
        return carry

    lax.fori_loop(0, total // TILE, mask_tile, 0)
    gacc[...] = jnp.zeros_like(gacc)

    def send_gy(i, carry):
        pltpu.make_async_remote_copy(
            src_ref=ysrc, dst_ref=gy.at[row], send_sem=gsend.at[1], recv_sem=grecv.at[1],
            device_id={"dp": (row + i) % ROWS * COLS + col}, device_id_type=MESH,
        ).start()
        return carry

    lax.fori_loop(1, ROWS, send_gy, 0)
    gy[row] = ysrc[...]

    wait_bytes(cot.at[:, 0], crecv.at[0])
    partner = 2 * chip + 1 - core
    forward = pltpu.make_async_remote_copy(
        src_ref=cot.at[:, core], dst_ref=cot.at[:, core], send_sem=csend.at[1], recv_sem=crecv.at[1],
        device_id={"seq": partner}, device_id_type=MESH,
    )
    forward.start()
    wait_bytes(gy.at[pl.ds(0, ROWS - 1)], grecv.at[1])
    summed = gy[0]
    for i in range(1, ROWS):
        summed = summed + gy[i]
    gains[...] = summed
    forward.wait()

    def live_block(i, carry):
        tokens = i * BLOCK + lax.broadcasted_iota(jnp.int32, (BLOCK, HEAD_DIM), 0)
        block = cot[i].reshape(BLOCK, HEAD_DIM).astype(jnp.float32)
        here = pl.ds(pl.multiple_of(i * BLOCK, BLOCK), BLOCK)
        live[here, :] = jnp.where(tokens < length, block, 0.0).astype(jnp.bfloat16)
        return carry

    lax.fori_loop(0, blocks, live_block, 0)
    gain_q, gain_k = gains[0:1, :], gains[1:2, :]

    def one_head(slot, carry):
        for index, (_, landing) in enumerate(arrays):
            wait_bytes(landing.at[slot], frecv.at[slot, index])

        def block_rows(i):
            return pl.ds(pl.multiple_of(i * BLOCK, BLOCK), BLOCK)

        def prepare(i, carry):
            here = block_rows(i)
            wide = xk[slot, here, :].astype(jnp.float32)
            norm = (wide * rms_inverse(wide) * gain_k).astype(jnp.bfloat16)
            ka[here, :HEAD_DIM] = norm
            kt[:, here] = norm.T
            wide = xq[slot, here, :].astype(jnp.float32)
            qa[here, :HEAD_DIM] = (wide * rms_inverse(wide) * gain_q).astype(jnp.bfloat16)
            zero = jnp.zeros((BLOCK, HEAD_DIM), jnp.float32)
            dk_acc[here, :] = zero
            dv_acc[here, :] = zero
            return carry

        lax.fori_loop(0, blocks, prepare, 0)

        nt = (((1,), (1,)), ((), ()))

        def query_block(b, carry):
            here = block_rows(b)
            q_block = qa[here, :]
            q_norm = q_block[:, :HEAD_DIM]
            live_rows = live[here, :]

            def scores(i, sums):
                den, mixed = sums
                keys = block_rows(i)
                logits = lax.dot_general(ka[keys, :], q_block, nt, preferred_element_type=jnp.float32)
                weight = jnp.exp(logits * FACTOR)
                grad = lax.dot_general(xv[slot, keys, :], live_rows, nt, preferred_element_type=jnp.float32)
                wbuf[keys, :] = weight
                gbuf[keys, :] = grad
                den = den + jnp.sum(weight, axis=0, keepdims=True)
                mixed = mixed + jnp.sum(weight * grad, axis=0, keepdims=True)
                return den, mixed

            zero = jnp.zeros((1, BLOCK), jnp.float32)
            den, mixed = lax.fori_loop(0, blocks, scores, (zero, zero))
            inv = 1.0 / den
            diag = mixed * inv

            def grads(i, dq_t):
                keys = block_rows(i)
                prob = wbuf[keys, :] * inv
                prob_low = prob.astype(jnp.bfloat16)
                grad_score = (prob * (gbuf[keys, :] - diag)).astype(jnp.bfloat16)
                dv_acc[keys, :] += jnp.dot(prob_low, live_rows, preferred_element_type=jnp.float32)
                dk_acc[keys, :] += jnp.dot(grad_score, q_norm, preferred_element_type=jnp.float32)
                return dq_t + jnp.dot(kt[:, keys], grad_score, preferred_element_type=jnp.float32)

            dq_t = lax.fori_loop(0, blocks, grads, jnp.zeros((HEAD_DIM, BLOCK), jnp.float32))
            upstream = (dq_t.T * FACTOR).astype(jnp.bfloat16).astype(jnp.float32)
            wide = xq[slot, here, :].astype(jnp.float32)
            grad, gain = rms_back(wide, rms_inverse(wide), gain_q, upstream)
            oq[slot, here, :] = grad
            gacc[0:1, :] += gain
            return carry

        if COMPUTE:
            lax.fori_loop(0, blocks, query_block, 0)

        def finish(i, carry):
            here = block_rows(i)
            upstream = (dk_acc[here, :] * FACTOR).astype(jnp.bfloat16).astype(jnp.float32)
            wide = xk[slot, here, :].astype(jnp.float32)
            grad, gain = rms_back(wide, rms_inverse(wide), gain_k, upstream)
            ok[slot, here, :] = grad
            ov[slot, here, :] = dv_acc[here, :].astype(jnp.bfloat16)
            gacc[1:2, :] += gain
            return carry

        lax.fori_loop(0, blocks, finish, 0)

        head = chip * per_chip + core + 2 * slot
        out_lanes = pl.ds(pl.multiple_of(head * HEAD_DIM, HEAD_DIM), HEAD_DIM)
        results = ((oq, dq_out), (ok, dk_out), (ov, dv_out))

        def give_back(target, core_to, local):
            other = 2 * target + core_to
            rows = pl.ds(pl.multiple_of(other * shard, shard), shard)
            for index, (source, landing) in enumerate(results):
                src = source.at[slot, rows, :]
                dst = landing.at[0, :, out_lanes]
                if local:
                    pltpu.make_async_copy(src, dst, orecv.at[index]).start()
                else:
                    pltpu.make_async_remote_copy(
                        src_ref=src, dst_ref=dst, send_sem=rsend.at[slot, index], recv_sem=orecv.at[index],
                        device_id={"seq": other}, device_id_type=MESH,
                    ).start()

        def back(i, carry):
            give_back(far(i), core, False)
            give_back(far(i), 1 - core, False)
            return carry

        lax.fori_loop(0, chips - 1, back, 0)
        give_back(chip, 1 - core, False)
        give_back(chip, core, True)
        return carry

    lax.fori_loop(0, 2 - core, one_head, 0)

    hsrc[...] = gacc[...]

    def send_hz(i, carry):
        pltpu.make_async_remote_copy(
            src_ref=hsrc, dst_ref=hz.at[seq], send_sem=gsend.at[2], recv_sem=grecv.at[2],
            device_id={"seq": (seq + i) % (2 * chips)}, device_id_type=MESH,
        ).start()
        return carry

    lax.fori_loop(1, 2 * chips, send_hz, 0)
    hz[seq] = hsrc[...]
    wait_bytes(hz.at[pl.ds(0, 2 * chips - 1)], grecv.at[2])
    summed = hz[0]
    for i in range(1, 2 * chips):
        summed = summed + hz[i]
    hsrc2[0] = summed

    def send_hx(i, carry):
        pltpu.make_async_remote_copy(
            src_ref=hsrc2.at[0], dst_ref=hx.at[col], send_sem=gsend.at[3], recv_sem=grecv.at[3],
            device_id={"dp": row * COLS + (col + i) % COLS}, device_id_type=MESH,
        ).start()
        return carry

    lax.fori_loop(1, COLS, send_hx, 0)
    hx[col] = summed
    wait_bytes(hx.at[pl.ds(0, COLS - 1)], grecv.at[3])
    summed = hx[0] + hx[1] + hx[2] + hx[3]
    hsrc2[1] = summed

    def send_hy(i, carry):
        pltpu.make_async_remote_copy(
            src_ref=hsrc2.at[1], dst_ref=hy.at[row], send_sem=gsend.at[4], recv_sem=grecv.at[4],
            device_id={"dp": (row + i) % ROWS * COLS + col}, device_id_type=MESH,
        ).start()
        return carry

    lax.fori_loop(1, ROWS, send_hy, 0)
    hy[row] = summed
    wait_bytes(hy.at[pl.ds(0, ROWS - 1)], grecv.at[4])
    summed = hy[0]
    for i in range(1, ROWS):
        summed = summed + hy[i]
    gain_out[...] = summed

    wait_bytes(gx.at[pl.ds(0, COLS - 1)], gsend.at[0])
    wait_bytes(gy.at[pl.ds(0, ROWS - 1)], gsend.at[1])
    wait_bytes(hz.at[pl.ds(0, 2 * chips - 1)], gsend.at[2])
    wait_bytes(hx.at[pl.ds(0, COLS - 1)], gsend.at[3])
    wait_bytes(hy.at[pl.ds(0, ROWS - 1)], gsend.at[4])
    wait_bytes(cot.at[pl.ds(0, chips - 1), 0], csend.at[0])
    count = chips * per_chip
    for index, (source, _) in enumerate(arrays):
        @pl.when(core == 0)
        def _():
            wait_bytes(source.at[0, :, pl.ds(0, (count - 2) * HEAD_DIM)], fsend.at[index])

        @pl.when(core == 1)
        def _():
            wait_bytes(source.at[0, :, pl.ds(0, (count - 1) * HEAD_DIM)], fsend.at[index])

    def sent(slot, carry):
        for index, buffer in enumerate((oq, ok, ov)):
            wait_bytes(buffer.at[slot, pl.ds(0, total - shard), :], rsend.at[slot, index])
        return carry

    lax.fori_loop(0, 2 - core, sent, 0)
    for index, out in enumerate((dq_out, dk_out, dv_out)):
        wait_bytes(out, orecv.at[index])


def body(queries, key_states, value_states, cotangent, norm_gains, tile_lists, clip_lengths):
    seq_count = lax.axis_size("seq")
    dp_count = lax.axis_size("dp")
    dp = lax.axis_index("dp")
    shard, width = queries.shape[1], queries.shape[2]
    heads = width // HEAD_DIM
    chips = seq_count // 2
    per_chip = heads // chips
    total = shard * seq_count
    owned = norm_gains.shape[1]
    lane = jnp.arange(HEAD_DIM, dtype=jnp.int32)
    spread = jnp.where(lane // owned == dp, jnp.tile(norm_gains, (1, dp_count)), 0.0)
    g_in = jnp.concatenate([spread, jnp.zeros((6, HEAD_DIM), jnp.float32)], 0)
    lists = jnp.tile(tile_lists.T, (1, HEAD_DIM // tile_lists.shape[0]))
    info = jnp.concatenate([lists, jnp.broadcast_to(clip_lengths[:, None], (4, HEAD_DIM))], 0)
    bf, f32 = jnp.bfloat16, jnp.float32
    hbm = pl.BlockSpec(memory_space=pl.ANY)
    vmem = pl.BlockSpec(memory_space=pltpu.VMEM)
    dma = pltpu.SemaphoreType.DMA
    shaped = jax.ShapeDtypeStruct(queries.shape, bf)
    pair = pltpu.VMEM((2, total, HEAD_DIM), bf)
    tiny = lambda n: pltpu.VMEM((n, 8, HEAD_DIM), f32)
    dq, dk, dv, gain_sum = pl.pallas_call(
        functools.partial(kernel, (chips, shard, per_chip)),
        out_shape=(shaped, shaped, shaped, jax.ShapeDtypeStruct((8, HEAD_DIM), f32)),
        in_specs=[hbm, hbm, hbm, hbm, vmem, vmem],
        out_specs=(hbm, hbm, hbm, vmem),
        scratch_shapes=[
            pair, pair, pair, pltpu.VMEM((chips, 2, shard, HEAD_DIM), bf), pair, pair, pair,
            pltpu.VMEM((total, 2 * HEAD_DIM), bf), pltpu.VMEM((total, 2 * HEAD_DIM), bf),
            pltpu.VMEM((HEAD_DIM, total), bf), pltpu.VMEM((total, HEAD_DIM), bf),
            pltpu.VMEM((total, BLOCK), f32), pltpu.VMEM((total, BLOCK), f32),
            pltpu.VMEM((total, HEAD_DIM), f32), pltpu.VMEM((total, HEAD_DIM), f32),
            tiny(COLS), tiny(ROWS), pltpu.VMEM((8, HEAD_DIM), f32), pltpu.VMEM((8, HEAD_DIM), f32),
            pltpu.VMEM((8, HEAD_DIM), f32), tiny(seq_count), tiny(COLS), tiny(ROWS),
            pltpu.VMEM((8, HEAD_DIM), f32), tiny(2),
            dma((3,)), dma((2, 3)), dma((2,)), dma((2,)), dma((2, 3)), dma((3,)), dma((5,)), dma((5,)),
        ],
        compiler_params=pltpu.CompilerParams(
            collective_id=0, has_side_effects=True, vmem_limit_bytes=48 * 1024 * 1024
        ),
    )(queries, key_states, value_states, cotangent, g_in, info)
    norm_factor = 1.0 / math.sqrt(dp_count * total * heads)
    gain_grad = lax.dynamic_slice_in_dim(gain_sum[:2], dp * owned, owned, 1) * norm_factor
    return dq, dk, dv, gain_grad


def solution(mesh):
    placed = (
        P("dp", "seq", None),
        P("dp", "seq", None),
        P("dp", "seq", None),
        P("dp", "seq", None),
        P(None, "dp"),
        P(),
        P("dp"),
    )
    return jax.shard_map(
        body,
        mesh=mesh,
        in_specs=placed,
        out_specs=(P("dp", "seq", None), P("dp", "seq", None), P("dp", "seq", None), P(None, "dp")),
        check_vma=False,
    )
```

```python
import functools
import math


import jax
import jax.numpy as jnp
from jax import lax
from jax.experimental import pallas as pl
from jax.experimental.pallas import tpu as pltpu
import ml_dtypes
from jax.sharding import PartitionSpec as P

HEAD_DIM = 128
TILE = 64
PIECES = 4
EPS = 1e-06
BLOCK = 256
MESH = pl.DeviceIdType.MESH
FACTOR = 1.0 / math.sqrt(HEAD_DIM)
BLOCKED = -30000.0
TWICE = math.log(2.0) / FACTOR


def wait_bytes(ref, sem):
    pltpu.make_async_copy(ref, ref, sem).wait()


def wait_many(ref, count, sem):
    if count:
        wait_bytes(ref.at[pl.ds(0, count)], sem)


def total_of(ref):
    total = ref[0]
    for i in range(1, ref.shape[0]):
        total = total + ref[i]
    return total


def rms_inverse(wide):
    return lax.rsqrt(jnp.mean(wide * wide, axis=-1, keepdims=True) + EPS)


def rms_back(wide, inverse, gain_row, upstream):
    scaled = upstream * gain_row
    inner = jnp.mean(wide * scaled, axis=-1, keepdims=True)
    grad = inverse * scaled - wide * (inverse * inverse * inverse * inner)
    return grad.astype(jnp.bfloat16), jnp.sum(upstream * wide * inverse, axis=0, keepdims=True)


def kernel(
    sizes,
    q_in, k_in, v_in, c_in, g_hbm, lists_hbm, lengths,
    dq_out, dk_out, dv_out, gain_out,
    xq, xk, xv, cot, oq, ok, ov,
    qa, ka, kt, live, wbuf, gbuf, dk_acc, dv_acc,
    gsrc, gx, gy, ysrc, gains, gacc, hz, hx, hy, hsrc, hsrc2,
    g_raw, lists, tsem,
    fsend, frecv, csend, crecv, osem, psem, rsend, orecv, gsend, grecv,
):
    chips, shard, per_chip, cols, rows = sizes
    seq = lax.axis_index("seq")
    dp = lax.axis_index("dp")
    chip, core = seq // 2, seq % 2
    row, col = dp // cols, dp % cols
    total = 2 * chips * shard
    blocks = total // BLOCK

    small = ((g_hbm, g_raw), (lists_hbm, lists))
    for index, (source, landing) in enumerate(small):
        pltpu.make_async_copy(source, landing, tsem.at[index]).start()

    barrier = pltpu.get_barrier_semaphore()

    def greet_seq(i, carry):
        pl.semaphore_signal(barrier, inc=1, device_id={"seq": (seq + i) % (2 * chips)}, device_id_type=MESH)
        return carry

    def greet_col(i, carry):
        pl.semaphore_signal(barrier, inc=1, device_id={"dp": row * cols + (col + i) % cols}, device_id_type=MESH)
        return carry

    def greet_row(i, carry):
        pl.semaphore_signal(barrier, inc=1, device_id={"dp": (row + i) % rows * cols + col}, device_id_type=MESH)
        return carry

    lax.fori_loop(1, 2 * chips, greet_seq, 0)
    lax.fori_loop(1, cols, greet_col, 0)
    lax.fori_loop(1, rows, greet_row, 0)
    pl.semaphore_wait(barrier, 2 * chips - 1 + cols - 1 + rows - 1)

    arrays = ((q_in, xq), (k_in, xk), (v_in, xv))
    my_rows = pl.ds(pl.multiple_of(seq * shard, shard), shard)

    def near(i):
        half = i // 2 + 1
        return (chip + half * (1 - 2 * (i % 2)) + chips) % chips

    def pass_on(origin, step, way, side):
        source = c_in.at[0] if step == 1 else cot.at[origin, core]
        pltpu.make_async_remote_copy(
            src_ref=source, dst_ref=cot.at[origin, core],
            send_sem=csend.at[side, step - 1], recv_sem=crecv.at[side, step - 1],
            device_id={"seq": 2 * ((chip + way + chips) % chips) + core}, device_id_type=MESH,
        ).start()

    def passed(step, side, sems):
        wait_bytes(cot.at[0, 0], sems.at[side, step - 1])

    own_cot = pltpu.make_async_copy(c_in.at[0], cot.at[chip, core], osem)
    own_cot.start()
    last_step = chips // 2

    def spread_head(which):
        owner, slot = which % 2, which // 2

        def to_chip(target, start_kind):
            lanes = pl.ds(pl.multiple_of((target * per_chip + which) * HEAD_DIM, HEAD_DIM), HEAD_DIM)
            for index, (source, landing) in enumerate(arrays):
                src = source.at[0, :, lanes]
                dst = landing.at[slot, my_rows, :]
                if start_kind == "local":
                    pltpu.make_async_copy(src, dst, frecv.at[slot, index]).start()
                else:
                    pltpu.make_async_remote_copy(
                        src_ref=src, dst_ref=dst, send_sem=fsend.at[index], recv_sem=frecv.at[slot, index],
                        device_id={"seq": 2 * target + owner}, device_id_type=MESH,
                    ).start()

        def remote(i, carry):
            to_chip(near(i), "remote")
            return carry

        def at_home():
            @pl.when(core == owner)
            def _():
                to_chip(chip, "local")

            @pl.when(core != owner)
            def _():
                to_chip(chip, "remote")

        return remote, at_home

    remote, at_home = spread_head(0)
    for step in range(1, last_step):
        for side, way in ((0, 1), (1, -1)):
            if step > 1:
                passed(step - 1, side, crecv)
            pass_on((chip - (step - 1) * way + chips) % chips, step, way, side)
        remote(2 * step - 2, 0)
        remote(2 * step - 1, 0)
    for side in range(2):
        passed(last_step - 1, side, crecv)
    way = 1 - 2 * core
    pass_on((chip - (last_step - 1) * way + chips) % chips, last_step, way, 0)
    remote(chips - 2, 0)
    at_home()
    for which in range(1, per_chip):
        remote, at_home = spread_head(which)
        lax.fori_loop(0, chips - 1, remote, 0)
        at_home()

    for index, (source, landing) in enumerate(small):
        pltpu.make_async_copy(source, landing, tsem.at[index]).wait()

    lane = lax.broadcasted_iota(jnp.int32, (8, HEAD_DIM), 1)
    sub = lax.broadcasted_iota(jnp.int32, (8, HEAD_DIM), 0)
    owned = g_raw.shape[1]
    spread = jnp.zeros((8, HEAD_DIM), jnp.float32)
    for r in range(2):
        for c in range(owned):
            spot = jnp.logical_and(sub == r, lane == dp * owned + c)
            spread = jnp.where(spot, g_raw[r, c], spread)
    gsrc[...] = spread

    lanes = lax.broadcasted_iota(jnp.int32, (TILE, HEAD_DIM), 1)
    places = lax.broadcasted_iota(jnp.int32, (TILE, HEAD_DIM), 0)
    length = lengths[0]
    high = float(ml_dtypes.bfloat16(TWICE))
    low = float(ml_dtypes.bfloat16(TWICE - high))

    def mask_tile(t, carry):
        named = jnp.zeros((TILE, HEAD_DIM), jnp.int32)
        for n in range(lists.shape[0]):
            named = named + (lanes % 32 == lists[n, t]).astype(jnp.int32)
        first = jnp.where(named > 0, jnp.where(named > 1, high, 0.0), BLOCKED)
        second = jnp.where(named > 1, low, 0.0)
        bias = jnp.where(lanes < 32, first, jnp.where(lanes < 64, second, 0.0))
        bias = jnp.where(lanes == 64, BLOCKED, bias)
        here = pl.ds(pl.multiple_of(t * TILE, TILE), TILE)
        qa[here, HEAD_DIM:] = bias.astype(jnp.bfloat16)
        mark = jnp.logical_and(lanes % 32 == t, lanes < 64)
        past = jnp.logical_and(lanes == 64, t * TILE + places >= length)
        ka[here, HEAD_DIM:] = jnp.where(jnp.logical_or(mark, past), 1.0, 0.0).astype(jnp.bfloat16)
        return carry

    lax.fori_loop(0, total // TILE, mask_tile, 0)
    def send_gx(i, carry):
        pltpu.make_async_remote_copy(
            src_ref=gsrc, dst_ref=gx.at[col], send_sem=gsend.at[0], recv_sem=grecv.at[0],
            device_id={"dp": row * cols + (col + i) % cols}, device_id_type=MESH,
        ).start()
        return carry

    lax.fori_loop(1, cols, send_gx, 0)
    gx[col] = gsrc[...]

    gacc[...] = jnp.zeros_like(gacc)
    wait_many(gx, cols - 1, grecv.at[0])
    ysrc[...] = total_of(gx)

    passed(last_step, 0, crecv)
    own_cot.wait()
    partner = 2 * chip + 1 - core
    forward = pltpu.make_async_remote_copy(
        src_ref=cot.at[:, core], dst_ref=cot.at[:, core], send_sem=psem.at[0], recv_sem=psem.at[1],
        device_id={"seq": partner}, device_id_type=MESH,
    )
    forward.start()
    def send_gy(i, carry):
        pltpu.make_async_remote_copy(
            src_ref=ysrc, dst_ref=gy.at[row], send_sem=gsend.at[1], recv_sem=grecv.at[1],
            device_id={"dp": (row + i) % rows * cols + col}, device_id_type=MESH,
        ).start()
        return carry

    lax.fori_loop(1, rows, send_gy, 0)
    gy[row] = ysrc[...]

    wait_many(gy, rows - 1, grecv.at[1])
    gains[...] = total_of(gy)
    forward.wait()

    def live_block(i, carry):
        tokens = i * BLOCK + lax.broadcasted_iota(jnp.int32, (BLOCK, HEAD_DIM), 0)
        block = cot[i].reshape(BLOCK, HEAD_DIM).astype(jnp.float32)
        here = pl.ds(pl.multiple_of(i * BLOCK, BLOCK), BLOCK)
        live[here, :] = jnp.where(tokens < length, block, 0.0).astype(jnp.bfloat16)
        return carry

    lax.fori_loop(0, blocks, live_block, 0)
    gain_q, gain_k = gains[0:1, :], gains[1:2, :]

    def one_head(slot, carry):
        for index, (_, landing) in enumerate(arrays):
            wait_bytes(landing.at[slot], frecv.at[slot, index])

        def block_rows(i):
            return pl.ds(pl.multiple_of(i * BLOCK, BLOCK), BLOCK)

        def prepare(i, carry):
            here = block_rows(i)
            wide = xk[slot, here, :].astype(jnp.float32)
            norm = (wide * rms_inverse(wide) * gain_k).astype(jnp.bfloat16)
            ka[here, :HEAD_DIM] = norm
            kt[:, here] = norm.T
            wide = xq[slot, here, :].astype(jnp.float32)
            qa[here, :HEAD_DIM] = (wide * rms_inverse(wide) * gain_q).astype(jnp.bfloat16)
            zero = jnp.zeros((BLOCK, HEAD_DIM), jnp.float32)
            dk_acc[here, :] = zero
            dv_acc[here, :] = zero
            return carry

        lax.fori_loop(0, blocks, prepare, 0, unroll=2)

        nt = (((1,), (1,)), ((), ()))

        def query_block(b, carry):
            here = block_rows(b)
            q_block = qa[here, :]
            q_norm = q_block[:, :HEAD_DIM]
            live_rows = live[here, :]

            def scores(i, sums):
                den, mixed = sums
                keys = block_rows(i)
                logits = lax.dot_general(ka[keys, :], q_block, nt, preferred_element_type=jnp.float32)
                weight = jnp.exp(logits * FACTOR)
                grad = lax.dot_general(xv[slot, keys, :], live_rows, nt, preferred_element_type=jnp.float32)
                wbuf[keys, :] = weight
                gbuf[keys, :] = grad
                den = den + jnp.sum(weight, axis=0, keepdims=True)
                mixed = mixed + jnp.sum(weight * grad, axis=0, keepdims=True)
                return den, mixed

            zero = jnp.zeros((1, BLOCK), jnp.float32)
            den, mixed = lax.fori_loop(0, blocks, scores, (zero, zero), unroll=True)
            inv = 1.0 / den
            diag = mixed * inv

            def grads(i, dq_t):
                keys = block_rows(i)
                prob = wbuf[keys, :] * inv
                prob_low = prob.astype(jnp.bfloat16)
                grad_score = (prob * (gbuf[keys, :] - diag)).astype(jnp.bfloat16)
                dv_acc[keys, :] += jnp.dot(prob_low, live_rows, preferred_element_type=jnp.float32)
                dk_acc[keys, :] += jnp.dot(grad_score, q_norm, preferred_element_type=jnp.float32)
                return dq_t + jnp.dot(kt[:, keys], grad_score, preferred_element_type=jnp.float32)

            dq_t = lax.fori_loop(
                0, blocks, grads, jnp.zeros((HEAD_DIM, BLOCK), jnp.float32), unroll=True
            )
            upstream = (dq_t.T * FACTOR).astype(jnp.bfloat16).astype(jnp.float32)
            wide = xq[slot, here, :].astype(jnp.float32)
            grad, gain = rms_back(wide, rms_inverse(wide), gain_q, upstream)
            oq[slot, here, :] = grad
            gacc[0:1, :] += gain
            return carry

        lax.fori_loop(0, blocks, query_block, 0)

        def finish(i, carry):
            here = block_rows(i)
            upstream = (dk_acc[here, :] * FACTOR).astype(jnp.bfloat16).astype(jnp.float32)
            wide = xk[slot, here, :].astype(jnp.float32)
            grad, gain = rms_back(wide, rms_inverse(wide), gain_k, upstream)
            ok[slot, here, :] = grad
            ov[slot, here, :] = dv_acc[here, :].astype(jnp.bfloat16)
            gacc[1:2, :] += gain
            return carry

        lax.fori_loop(0, blocks, finish, 0, unroll=2)

        @pl.when(slot == 1 - core)
        def _():
            hsrc[...] = gacc[...]
            hz[seq] = gacc[...]

        head = chip * per_chip + core + 2 * slot
        out_lanes = pl.ds(pl.multiple_of(head * HEAD_DIM, HEAD_DIM), HEAD_DIM)
        results = ((oq, dq_out), (ok, dk_out), (ov, dv_out))

        def give_back(target, core_to, local):
            other = 2 * target + core_to
            rows = pl.ds(pl.multiple_of(other * shard, shard), shard)
            for index, (source, landing) in enumerate(results):
                src = source.at[slot, rows, :]
                dst = landing.at[0, :, out_lanes]
                if local:
                    pltpu.make_async_copy(src, dst, orecv.at[index]).start()
                else:
                    pltpu.make_async_remote_copy(
                        src_ref=src, dst_ref=dst, send_sem=rsend.at[slot, index], recv_sem=orecv.at[index],
                        device_id={"seq": other}, device_id_type=MESH,
                    ).start()

        def back(i, carry):
            give_back(near(i), core, False)
            give_back(near(i), 1 - core, False)
            return carry

        lax.fori_loop(0, 2, back, 0)

        @pl.when(slot == 1 - core)
        def _():
            def send_hz(i, carry):
                pltpu.make_async_remote_copy(
                    src_ref=hsrc, dst_ref=hz.at[seq], send_sem=gsend.at[2], recv_sem=grecv.at[2],
                    device_id={"seq": (seq + i) % (2 * chips)}, device_id_type=MESH,
                ).start()
                return carry

            lax.fori_loop(1, 2 * chips, send_hz, 0)

        lax.fori_loop(2, chips - 1, back, 0)
        give_back(chip, 1 - core, False)
        give_back(chip, core, True)
        return carry

    lax.fori_loop(0, 2 - core, one_head, 0)

    wait_many(hz, 2 * chips - 1, grecv.at[2])
    summed = total_of(hz)
    hsrc2[0] = summed

    def send_hx(i, carry):
        pltpu.make_async_remote_copy(
            src_ref=hsrc2.at[0], dst_ref=hx.at[col], send_sem=gsend.at[3], recv_sem=grecv.at[3],
            device_id={"dp": row * cols + (col + i) % cols}, device_id_type=MESH,
        ).start()
        return carry

    lax.fori_loop(1, cols, send_hx, 0)
    hx[col] = summed
    wait_many(hx, cols - 1, grecv.at[3])
    summed = total_of(hx)
    hsrc2[1] = summed

    def send_hy(i, carry):
        pltpu.make_async_remote_copy(
            src_ref=hsrc2.at[1], dst_ref=hy.at[row], send_sem=gsend.at[4], recv_sem=grecv.at[4],
            device_id={"dp": (row + i) % rows * cols + col}, device_id_type=MESH,
        ).start()
        return carry

    lax.fori_loop(1, rows, send_hy, 0)
    hy[row] = summed
    wait_many(hy, rows - 1, grecv.at[4])
    gain_out[...] = total_of(hy)

    wait_many(gx, cols - 1, gsend.at[0])
    wait_many(gy, rows - 1, gsend.at[1])
    wait_many(hz, 2 * chips - 1, gsend.at[2])
    wait_many(hx, cols - 1, gsend.at[3])
    wait_many(hy, rows - 1, gsend.at[4])
    for step in range(1, last_step):
        passed(step, 0, csend)
        passed(step, 1, csend)
    passed(last_step, 0, csend)
    count = chips * per_chip
    for index, (source, _) in enumerate(arrays):
        @pl.when(core == 0)
        def _():
            wait_bytes(source.at[0, :, pl.ds(0, (count - 2) * HEAD_DIM)], fsend.at[index])

        @pl.when(core == 1)
        def _():
            wait_bytes(source.at[0, :, pl.ds(0, (count - 1) * HEAD_DIM)], fsend.at[index])

    def sent(slot, carry):
        for index, buffer in enumerate((oq, ok, ov)):
            wait_bytes(buffer.at[slot, pl.ds(0, total - shard), :], rsend.at[slot, index])
        return carry

    lax.fori_loop(0, 2 - core, sent, 0)
    for index, out in enumerate((dq_out, dk_out, dv_out)):
        wait_bytes(out, orecv.at[index])


def deliver(q_ref, k_ref, v_ref, gain_hbm, q_out, k_out, v_out, gain_out_hbm, held, gain_ref, gain_out, taken, given, gsem):
    shard = q_ref.shape[1]
    piece = shard // PIECES
    pairs = ((q_ref, q_out), (k_ref, k_out), (v_ref, v_out))

    def take(index, part):
        span = pl.ds(part * piece, piece)
        return pltpu.make_async_copy(pairs[index][0].at[0, span], held.at[index, span], taken.at[index, part])

    def give(index, part):
        span = pl.ds(part * piece, piece)
        return pltpu.make_async_copy(held.at[index, span], pairs[index][1].at[0, span], given.at[index, part])

    places = [(index, part) for index in range(3) for part in range(PIECES)]
    gain_take = pltpu.make_async_copy(gain_hbm, gain_ref, gsem.at[0])
    gain_give = pltpu.make_async_copy(gain_out, gain_out_hbm, gsem.at[1])
    gain_take.start()
    for place in places:
        take(*place).start()
    gain_take.wait()
    owned = gain_out.shape[1]
    turned = pltpu.roll(gain_ref[...], HEAD_DIM - lax.axis_index("dp") * owned, 1)
    count = lax.axis_size("dp") * lax.axis_size("seq") * shard * (q_ref.shape[2] // HEAD_DIM)
    gain_out[...] = turned[:2, :owned] * (1.0 / math.sqrt(count))
    for place in places:
        take(*place).wait()
        give(*place).start()
    gain_give.start()
    for place in places:
        give(*place).wait()
    gain_give.wait()


def body(queries, key_states, value_states, cotangent, norm_gains, tile_lists, clip_lengths):
    seq_count = lax.axis_size("seq")
    dp_count = lax.axis_size("dp")
    dp = lax.axis_index("dp")
    shard, width = queries.shape[1], queries.shape[2]
    heads = width // HEAD_DIM
    chips = seq_count // 2
    per_chip = heads // chips
    total = shard * seq_count
    owned = norm_gains.shape[1]
    cols = math.gcd(dp_count, 4)
    rows = dp_count // cols
    bf, f32 = jnp.bfloat16, jnp.float32
    hbm = pl.BlockSpec(memory_space=pltpu.HBM)
    vmem = pl.BlockSpec(memory_space=pltpu.VMEM)
    dma = pltpu.SemaphoreType.DMA
    shaped = jax.ShapeDtypeStruct(queries.shape, bf)
    pair = pltpu.VMEM((2, total, HEAD_DIM), bf)
    tiny = lambda n: pltpu.VMEM((n, 8, HEAD_DIM), f32)
    dq, dk, dv, gain_sum = pl.pallas_call(
        functools.partial(kernel, (chips, shard, per_chip, cols, rows)),
        out_shape=(shaped, shaped, shaped, jax.ShapeDtypeStruct((8, HEAD_DIM), f32)),
        in_specs=[hbm] * 6 + [pl.BlockSpec(memory_space=pltpu.SMEM)],
        out_specs=(hbm, hbm, hbm, vmem),
        scratch_shapes=[
            pair, pair, pair, pltpu.VMEM((chips, 2, shard, HEAD_DIM), bf), pair, pair, pair,
            pltpu.VMEM((total, 2 * HEAD_DIM), bf), pltpu.VMEM((total, 2 * HEAD_DIM), bf),
            pltpu.VMEM((HEAD_DIM, total), bf), pltpu.VMEM((total, HEAD_DIM), bf),
            pltpu.VMEM((total, BLOCK), f32), pltpu.VMEM((total, BLOCK), f32),
            pltpu.VMEM((total, HEAD_DIM), f32), pltpu.VMEM((total, HEAD_DIM), f32),
            pltpu.VMEM((8, HEAD_DIM), f32), tiny(cols), tiny(rows), pltpu.VMEM((8, HEAD_DIM), f32),
            pltpu.VMEM((8, HEAD_DIM), f32),
            pltpu.VMEM((8, HEAD_DIM), f32), tiny(seq_count), tiny(cols), tiny(rows),
            pltpu.VMEM((8, HEAD_DIM), f32), tiny(2),
            pltpu.SMEM(norm_gains.shape, f32), pltpu.SMEM(tile_lists.T.shape, jnp.int32),
            dma((2,)),
            dma((3,)), dma((2, 3)), dma((2, chips // 2)), dma((2, chips // 2)), dma(()), dma((2,)), dma((2, 3)), dma((3,)), dma((5,)), dma((5,)),
        ],
        compiler_params=pltpu.CompilerParams(
            collective_id=0, has_side_effects=True, vmem_limit_bytes=63 * 1024 * 1024
        ),
    )(
        queries, key_states, value_states, cotangent, norm_gains, tile_lists.T, clip_lengths
    )
    return pl.pallas_call(
        deliver,
        out_shape=(shaped, shaped, shaped, jax.ShapeDtypeStruct(norm_gains.shape, f32)),
        in_specs=[hbm] * 4,
        out_specs=(hbm,) * 4,
        scratch_shapes=[
            pltpu.VMEM((3, shard, width), bf), pltpu.VMEM((8, HEAD_DIM), f32), pltpu.VMEM(norm_gains.shape, f32),
            dma((3, PIECES)), dma((3, PIECES)), dma((2,)),
        ],
        compiler_params=pltpu.CompilerParams(vmem_limit_bytes=63 * 1024 * 1024),
    )(dq, dk, dv, gain_sum)


def solution(mesh):
    placed = (
        P("dp", "seq", None),
        P("dp", "seq", None),
        P("dp", "seq", None),
        P("dp", "seq", None),
        P(None, "dp"),
        P(),
        P("dp"),
    )
    return jax.shard_map(
        body,
        mesh=mesh,
        in_specs=placed,
        out_specs=(P("dp", "seq", None), P("dp", "seq", None), P("dp", "seq", None), P(None, "dp")),
        check_vma=False,
    )
```

```python
import functools
import math


import jax
import jax.numpy as jnp
from jax import lax
from jax.experimental import pallas as pl
from jax.experimental.pallas import tpu as pltpu
import ml_dtypes
from jax.sharding import PartitionSpec as P

HEAD_DIM = 128
TILE = 64
EPS = 1e-06
BLOCK = 256
MESH = pl.DeviceIdType.MESH
FACTOR = 1.0 / math.sqrt(HEAD_DIM)
BLOCKED = -30000.0
TWICE = math.log(2.0) / FACTOR


def wait_bytes(ref, sem):
    pltpu.make_async_copy(ref, ref, sem).wait()


def wait_many(ref, count, sem):
    if count:
        wait_bytes(ref.at[pl.ds(0, count)], sem)


def total_of(ref):
    total = ref[0]
    for i in range(1, ref.shape[0]):
        total = total + ref[i]
    return total


def rms_inverse(wide):
    return lax.rsqrt(jnp.mean(wide * wide, axis=-1, keepdims=True) + EPS)


def rms_back(wide, inverse, gain_row, upstream):
    scaled = upstream * gain_row
    inner = jnp.mean(wide * scaled, axis=-1, keepdims=True)
    grad = inverse * scaled - wide * (inverse * inverse * inverse * inner)
    return grad.astype(jnp.bfloat16), jnp.sum(upstream * wide * inverse, axis=0, keepdims=True)


def kernel(
    sizes,
    q_in, k_in, v_in, c_in, g_hbm, lists_hbm, lengths,
    dq_out, dk_out, dv_out, gain_out,
    xq, xk, xv, cot, oq, ok, ov,
    qa, ka, kt, live, wbuf, gbuf, dk_acc, dv_acc,
    gsrc, gx, gy, ysrc, gains, gacc, hz, hx, hy, hsrc, hsrc2, hsum,
    g_raw, lists, tsem,
    fsend, frecv, csend, crecv, osem, psem, rsend, orecv, gsend, grecv,
):
    chips, shard, per_chip, cols, rows = sizes
    seq = lax.axis_index("seq")
    dp = lax.axis_index("dp")
    chip, core = seq // 2, seq % 2
    row, col = dp // cols, dp % cols
    total = 2 * chips * shard
    blocks = total // BLOCK

    small = ((g_hbm, g_raw), (lists_hbm, lists))
    for index, (source, landing) in enumerate(small):
        pltpu.make_async_copy(source, landing, tsem.at[index]).start()

    barrier = pltpu.get_barrier_semaphore()

    def greet_seq(i, carry):
        pl.semaphore_signal(barrier, inc=1, device_id={"seq": (seq + i) % (2 * chips)}, device_id_type=MESH)
        return carry

    def greet_col(i, carry):
        pl.semaphore_signal(barrier, inc=1, device_id={"dp": row * cols + (col + i) % cols}, device_id_type=MESH)
        return carry

    def greet_row(i, carry):
        pl.semaphore_signal(barrier, inc=1, device_id={"dp": (row + i) % rows * cols + col}, device_id_type=MESH)
        return carry

    lax.fori_loop(1, 2 * chips, greet_seq, 0)

    hub = 1
    is_hub = seq == hub

    @pl.when(is_hub)
    def _():
        lax.fori_loop(1, cols, greet_col, 0)
        lax.fori_loop(1, rows, greet_row, 0)

    for index, (source, landing) in enumerate(small):
        pltpu.make_async_copy(source, landing, tsem.at[index]).wait()

    lane = lax.broadcasted_iota(jnp.int32, (8, HEAD_DIM), 1)
    sub = lax.broadcasted_iota(jnp.int32, (8, HEAD_DIM), 0)
    owned = g_raw.shape[1]
    spread = jnp.zeros((8, HEAD_DIM), jnp.float32)
    for r in range(2):
        for c in range(owned):
            spot = jnp.logical_and(sub == r, lane == dp * owned + c)
            spread = jnp.where(spot, g_raw[r, c], spread)
    gsrc[...] = spread

    @pl.when(is_hub)
    def _():
        pl.semaphore_wait(barrier, 2 * chips - 1 + cols - 1 + rows - 1)

    @pl.when(seq != hub)
    def _():
        pl.semaphore_wait(barrier, 2 * chips - 1)

    def send_gx(i, carry):
        pltpu.make_async_remote_copy(
            src_ref=gsrc, dst_ref=gx.at[col], send_sem=gsend.at[0], recv_sem=grecv.at[0],
            device_id={"dp": row * cols + (col + i) % cols}, device_id_type=MESH,
        ).start()
        return carry

    def send_gy(i, carry):
        pltpu.make_async_remote_copy(
            src_ref=ysrc, dst_ref=gy.at[row], send_sem=gsend.at[1], recv_sem=grecv.at[1],
            device_id={"dp": (row + i) % rows * cols + col}, device_id_type=MESH,
        ).start()
        return carry

    def send_gains(i, carry):
        pltpu.make_async_remote_copy(
            src_ref=gains, dst_ref=gains, send_sem=gsend.at[5], recv_sem=grecv.at[5],
            device_id={"seq": (seq + i) % (2 * chips)}, device_id_type=MESH,
        ).start()
        return carry

    @pl.when(is_hub)
    def _():
        lax.fori_loop(1, cols, send_gx, 0)
        gx[col] = gsrc[...]


    arrays = ((q_in, xq), (k_in, xk), (v_in, xv))
    my_rows = pl.ds(pl.multiple_of(seq * shard, shard), shard)

    def near(i):
        half = i // 2 + 1
        return (chip + half * (1 - 2 * (i % 2)) + chips) % chips

    def pass_on(origin, step, way, side):
        source = c_in.at[0] if step == 1 else cot.at[origin, core]
        pltpu.make_async_remote_copy(
            src_ref=source, dst_ref=cot.at[origin, core],
            send_sem=csend.at[side, step - 1], recv_sem=crecv.at[side, step - 1],
            device_id={"seq": 2 * ((chip + way + chips) % chips) + core}, device_id_type=MESH,
        ).start()

    def passed(step, side, sems):
        wait_bytes(cot.at[0, 0], sems.at[side, step - 1])

    own_cot = pltpu.make_async_copy(c_in.at[0], cot.at[chip, core], osem)
    own_cot.start()
    last_step = chips // 2

    def spread_head(which):
        owner, slot = which % 2, which // 2

        def to_chip(target, start_kind):
            lanes = pl.ds(pl.multiple_of((target * per_chip + which) * HEAD_DIM, HEAD_DIM), HEAD_DIM)
            for index, (source, landing) in enumerate(arrays):
                src = source.at[0, :, lanes]
                dst = landing.at[slot, my_rows, :]
                if start_kind == "local":
                    pltpu.make_async_copy(src, dst, frecv.at[slot, index]).start()
                else:
                    pltpu.make_async_remote_copy(
                        src_ref=src, dst_ref=dst, send_sem=fsend.at[index], recv_sem=frecv.at[slot, index],
                        device_id={"seq": 2 * target + owner}, device_id_type=MESH,
                    ).start()

        def remote(i, carry):
            to_chip(near(i), "remote")
            return carry

        def at_home():
            @pl.when(core == owner)
            def _():
                to_chip(chip, "local")

            @pl.when(core != owner)
            def _():
                to_chip(chip, "remote")

        return remote, at_home

    remote, at_home = spread_head(0)
    for step in range(1, last_step):
        for side, way in ((0, 1), (1, -1)):
            if step > 1:
                passed(step - 1, side, crecv)
            pass_on((chip - (step - 1) * way + chips) % chips, step, way, side)
        remote(2 * step - 2, 0)
        remote(2 * step - 1, 0)
    for side in range(2):
        passed(last_step - 1, side, crecv)
    way = 1 - 2 * core
    pass_on((chip - (last_step - 1) * way + chips) % chips, last_step, way, 0)
    remote(chips - 2, 0)
    at_home()
    lanes = lax.broadcasted_iota(jnp.int32, (TILE, HEAD_DIM), 1)
    places = lax.broadcasted_iota(jnp.int32, (TILE, HEAD_DIM), 0)
    length = lengths[0]
    high = float(ml_dtypes.bfloat16(TWICE))
    low = float(ml_dtypes.bfloat16(TWICE - high))

    def mask_tile(t, carry):
        named = jnp.zeros((TILE, HEAD_DIM), jnp.int32)
        for n in range(lists.shape[0]):
            named = named + (lanes % 32 == lists[n, t]).astype(jnp.int32)
        first = jnp.where(named > 0, jnp.where(named > 1, high, 0.0), BLOCKED)
        second = jnp.where(named > 1, low, 0.0)
        bias = jnp.where(lanes < 32, first, jnp.where(lanes < 64, second, 0.0))
        bias = jnp.where(lanes == 64, BLOCKED, bias)
        here = pl.ds(pl.multiple_of(t * TILE, TILE), TILE)
        qa[here, HEAD_DIM:] = bias.astype(jnp.bfloat16)
        mark = jnp.logical_and(lanes % 32 == t, lanes < 64)
        past = jnp.logical_and(lanes == 64, t * TILE + places >= length)
        ka[here, HEAD_DIM:] = jnp.where(jnp.logical_or(mark, past), 1.0, 0.0).astype(jnp.bfloat16)
        return carry

    tiles = total // TILE

    @pl.when(is_hub)
    def _():
        wait_many(gx, cols - 1, grecv.at[0])
        ysrc[...] = total_of(gx)

    lax.fori_loop(0, tiles // 2, mask_tile, 0)

    @pl.when(is_hub)
    def _():
        lax.fori_loop(1, rows, send_gy, 0)
        gy[row] = ysrc[...]
        wait_many(gy, rows - 1, grecv.at[1])
        gains[...] = total_of(gy)

    lax.fori_loop(tiles // 2, tiles, mask_tile, 0)
    gacc[...] = jnp.zeros_like(gacc)

    @pl.when(is_hub)
    def _():
        lax.fori_loop(1, 2 * chips, send_gains, 0)

    for which in range(1, per_chip):
        remote, at_home = spread_head(which)
        lax.fori_loop(0, chips - 1, remote, 0)
        at_home()

    passed(last_step, 0, crecv)
    own_cot.wait()
    partner = 2 * chip + 1 - core
    forward = pltpu.make_async_remote_copy(
        src_ref=cot.at[:, core], dst_ref=cot.at[:, core], send_sem=psem.at[0], recv_sem=psem.at[1],
        device_id={"seq": partner}, device_id_type=MESH,
    )
    forward.start()
    forward.wait()

    @pl.when(seq != hub)
    def _():
        wait_bytes(gains, grecv.at[5])


    def live_block(i, carry):
        tokens = i * BLOCK + lax.broadcasted_iota(jnp.int32, (BLOCK, HEAD_DIM), 0)
        block = cot[i].reshape(BLOCK, HEAD_DIM).astype(jnp.float32)
        here = pl.ds(pl.multiple_of(i * BLOCK, BLOCK), BLOCK)
        live[here, :] = jnp.where(tokens < length, block, 0.0).astype(jnp.bfloat16)
        return carry

    lax.fori_loop(0, blocks, live_block, 0)
    gain_q, gain_k = gains[0:1, :], gains[1:2, :]

    def one_head(slot, carry):
        for index, (_, landing) in enumerate(arrays):
            wait_bytes(landing.at[slot], frecv.at[slot, index])

        def block_rows(i):
            return pl.ds(pl.multiple_of(i * BLOCK, BLOCK), BLOCK)

        def prepare(i, carry):
            here = block_rows(i)
            wide = xk[slot, here, :].astype(jnp.float32)
            norm = (wide * rms_inverse(wide) * gain_k).astype(jnp.bfloat16)
            ka[here, :HEAD_DIM] = norm
            kt[:, here] = norm.T
            wide = xq[slot, here, :].astype(jnp.float32)
            qa[here, :HEAD_DIM] = (wide * rms_inverse(wide) * gain_q).astype(jnp.bfloat16)
            zero = jnp.zeros((BLOCK, HEAD_DIM), jnp.float32)
            dk_acc[here, :] = zero
            dv_acc[here, :] = zero
            return carry

        lax.fori_loop(0, blocks, prepare, 0, unroll=2)

        nt = (((1,), (1,)), ((), ()))

        def query_block(b, carry):
            here = block_rows(b)
            q_block = qa[here, :]
            q_norm = q_block[:, :HEAD_DIM]
            live_rows = live[here, :]

            def scores(i, sums):
                den, mixed = sums
                keys = block_rows(i)
                logits = lax.dot_general(ka[keys, :], q_block, nt, preferred_element_type=jnp.float32)
                weight = jnp.exp(logits * FACTOR)
                grad = lax.dot_general(xv[slot, keys, :], live_rows, nt, preferred_element_type=jnp.float32)
                wbuf[keys, :] = weight
                gbuf[keys, :] = grad
                den = den + jnp.sum(weight, axis=0, keepdims=True)
                mixed = mixed + jnp.sum(weight * grad, axis=0, keepdims=True)
                return den, mixed

            zero = jnp.zeros((1, BLOCK), jnp.float32)
            den, mixed = lax.fori_loop(0, blocks, scores, (zero, zero), unroll=True)
            inv = 1.0 / den
            diag = mixed * inv

            def grads(i, dq_t):
                keys = block_rows(i)
                prob = wbuf[keys, :] * inv
                prob_low = prob.astype(jnp.bfloat16)
                grad_score = (prob * (gbuf[keys, :] - diag)).astype(jnp.bfloat16)
                dv_acc[keys, :] += jnp.dot(prob_low, live_rows, preferred_element_type=jnp.float32)
                dk_acc[keys, :] += jnp.dot(grad_score, q_norm, preferred_element_type=jnp.float32)
                return dq_t + jnp.dot(kt[:, keys], grad_score, preferred_element_type=jnp.float32)

            dq_t = lax.fori_loop(
                0, blocks, grads, jnp.zeros((HEAD_DIM, BLOCK), jnp.float32), unroll=True
            )
            upstream = (dq_t.T * FACTOR).astype(jnp.bfloat16).astype(jnp.float32)
            wide = xq[slot, here, :].astype(jnp.float32)
            grad, gain = rms_back(wide, rms_inverse(wide), gain_q, upstream)
            oq[slot, here, :] = grad
            gacc[0:1, :] += gain
            return carry

        lax.fori_loop(0, blocks, query_block, 0)

        def finish(i, carry):
            here = block_rows(i)
            upstream = (dk_acc[here, :] * FACTOR).astype(jnp.bfloat16).astype(jnp.float32)
            wide = xk[slot, here, :].astype(jnp.float32)
            grad, gain = rms_back(wide, rms_inverse(wide), gain_k, upstream)
            ok[slot, here, :] = grad
            ov[slot, here, :] = dv_acc[here, :].astype(jnp.bfloat16)
            gacc[1:2, :] += gain
            return carry

        lax.fori_loop(0, blocks, finish, 0, unroll=2)

        @pl.when(slot == 1 - core)
        def _():
            hsrc[...] = gacc[...]
            hz[seq] = gacc[...]

        head = chip * per_chip + core + 2 * slot
        out_lanes = pl.ds(pl.multiple_of(head * HEAD_DIM, HEAD_DIM), HEAD_DIM)
        results = ((oq, dq_out), (ok, dk_out), (ov, dv_out))

        def give_back(target, core_to, local):
            other = 2 * target + core_to
            rows = pl.ds(pl.multiple_of(other * shard, shard), shard)
            for index, (source, landing) in enumerate(results):
                src = source.at[slot, rows, :]
                dst = landing.at[0, :, out_lanes]
                if local:
                    pltpu.make_async_copy(src, dst, orecv.at[index]).start()
                else:
                    pltpu.make_async_remote_copy(
                        src_ref=src, dst_ref=dst, send_sem=rsend.at[slot, index], recv_sem=orecv.at[index],
                        device_id={"seq": other}, device_id_type=MESH,
                    ).start()

        def back(i, carry):
            give_back(near(i), core, False)
            give_back(near(i), 1 - core, False)
            return carry

        lax.fori_loop(0, 2, back, 0)

        @pl.when(jnp.logical_and(slot == 1 - core, seq != hub))
        def _():
            pltpu.make_async_remote_copy(
                src_ref=hsrc, dst_ref=hz.at[seq], send_sem=gsend.at[2], recv_sem=grecv.at[2],
                device_id={"seq": hub}, device_id_type=MESH,
            ).start()

        lax.fori_loop(2, chips - 1, back, 0)
        give_back(chip, 1 - core, False)
        give_back(chip, core, True)
        return carry

    lax.fori_loop(0, 2 - core, one_head, 0)

    def send_hx(i, carry):
        pltpu.make_async_remote_copy(
            src_ref=hsrc2.at[0], dst_ref=hx.at[col], send_sem=gsend.at[3], recv_sem=grecv.at[3],
            device_id={"dp": row * cols + (col + i) % cols}, device_id_type=MESH,
        ).start()
        return carry

    def send_hy(i, carry):
        pltpu.make_async_remote_copy(
            src_ref=hsrc2.at[1], dst_ref=hy.at[row], send_sem=gsend.at[4], recv_sem=grecv.at[4],
            device_id={"dp": (row + i) % rows * cols + col}, device_id_type=MESH,
        ).start()
        return carry

    def send_total(i, carry):
        pltpu.make_async_remote_copy(
            src_ref=hsum, dst_ref=hsum, send_sem=gsend.at[6], recv_sem=grecv.at[6],
            device_id={"seq": (seq + i) % (2 * chips)}, device_id_type=MESH,
        ).start()
        return carry

    @pl.when(is_hub)
    def _():
        wait_many(hz, 2 * chips - 1, grecv.at[2])
        summed = total_of(hz)
        hsrc2[0] = summed
        hx[col] = summed
        lax.fori_loop(1, cols, send_hx, 0)
        wait_many(hx, cols - 1, grecv.at[3])
        summed = total_of(hx)
        hsrc2[1] = summed
        hy[row] = summed
        lax.fori_loop(1, rows, send_hy, 0)
        wait_many(hy, rows - 1, grecv.at[4])
        hsum[...] = total_of(hy)
        lax.fori_loop(1, 2 * chips, send_total, 0)
        wait_many(gx, cols - 1, gsend.at[0])
        wait_many(gy, rows - 1, gsend.at[1])
        wait_many(hx, cols - 1, gsend.at[3])
        wait_many(hy, rows - 1, gsend.at[4])
        wait_many(hz, 2 * chips - 1, gsend.at[5])
        wait_many(hz, 2 * chips - 1, gsend.at[6])

    @pl.when(seq != hub)
    def _():
        wait_bytes(hsrc, gsend.at[2])
        wait_bytes(hsum, grecv.at[6])

    gain_out[...] = hsum[...]

    for step in range(1, last_step):
        passed(step, 0, csend)
        passed(step, 1, csend)
    passed(last_step, 0, csend)
    count = chips * per_chip
    for index, (source, _) in enumerate(arrays):
        @pl.when(core == 0)
        def _():
            wait_bytes(source.at[0, :, pl.ds(0, (count - 2) * HEAD_DIM)], fsend.at[index])

        @pl.when(core == 1)
        def _():
            wait_bytes(source.at[0, :, pl.ds(0, (count - 1) * HEAD_DIM)], fsend.at[index])

    def sent(slot, carry):
        for index, buffer in enumerate((oq, ok, ov)):
            wait_bytes(buffer.at[slot, pl.ds(0, total - shard), :], rsend.at[slot, index])
        return carry

    lax.fori_loop(0, 2 - core, sent, 0)
    for index, out in enumerate((dq_out, dk_out, dv_out)):
        wait_bytes(out, orecv.at[index])


def deliver(q_ref, k_ref, v_ref, gain_ref, q_out, k_out, v_out, gain_hbm, gain_out, sems):
    copies = [
        pltpu.make_async_copy(source, out, sems.at[index])
        for index, (source, out) in enumerate(((q_ref, q_out), (k_ref, k_out), (v_ref, v_out)))
    ]
    for copy in copies:
        copy.start()
    owned = gain_out.shape[1]
    turned = pltpu.roll(gain_ref[...], HEAD_DIM - lax.axis_index("dp") * owned, 1)
    count = lax.axis_size("dp") * lax.axis_size("seq") * q_ref.shape[1] * (q_ref.shape[2] // HEAD_DIM)
    gain_out[...] = turned[:2, :owned] * (1.0 / math.sqrt(count))
    copies.append(pltpu.make_async_copy(gain_out, gain_hbm, sems.at[3]))
    copies[3].start()
    for copy in copies:
        copy.wait()


def body(queries, key_states, value_states, cotangent, norm_gains, tile_lists, clip_lengths):
    seq_count = lax.axis_size("seq")
    dp_count = lax.axis_size("dp")
    dp = lax.axis_index("dp")
    shard, width = queries.shape[1], queries.shape[2]
    heads = width // HEAD_DIM
    chips = seq_count // 2
    per_chip = heads // chips
    total = shard * seq_count
    owned = norm_gains.shape[1]
    cols = math.gcd(dp_count, 4)
    rows = dp_count // cols
    bf, f32 = jnp.bfloat16, jnp.float32
    hbm = pl.BlockSpec(memory_space=pltpu.HBM)
    vmem = pl.BlockSpec(memory_space=pltpu.VMEM)
    dma = pltpu.SemaphoreType.DMA
    shaped = jax.ShapeDtypeStruct(queries.shape, bf)
    pair = pltpu.VMEM((2, total, HEAD_DIM), bf)
    tiny = lambda n: pltpu.VMEM((n, 8, HEAD_DIM), f32)
    fixed = (queries, key_states, value_states, cotangent, norm_gains, tile_lists.T)
    dq, dk, dv, gain_sum = pl.pallas_call(
        functools.partial(kernel, (chips, shard, per_chip, cols, rows)),
        out_shape=(shaped, shaped, shaped, jax.ShapeDtypeStruct((8, HEAD_DIM), f32)),
        in_specs=[hbm] * 6 + [pl.BlockSpec(memory_space=pltpu.SMEM)],
        out_specs=(vmem, vmem, vmem, vmem),
        scratch_shapes=[
            pair, pair, pair, pltpu.VMEM((chips, 2, shard, HEAD_DIM), bf), pair, pair, pair,
            pltpu.VMEM((total, 2 * HEAD_DIM), bf), pltpu.VMEM((total, 2 * HEAD_DIM), bf),
            pltpu.VMEM((HEAD_DIM, total), bf), pltpu.VMEM((total, HEAD_DIM), bf),
            pltpu.VMEM((total, BLOCK), f32), pltpu.VMEM((total, BLOCK), f32),
            pltpu.VMEM((total, HEAD_DIM), f32), pltpu.VMEM((total, HEAD_DIM), f32),
            pltpu.VMEM((8, HEAD_DIM), f32), tiny(cols), tiny(rows), pltpu.VMEM((8, HEAD_DIM), f32),
            pltpu.VMEM((8, HEAD_DIM), f32),
            pltpu.VMEM((8, HEAD_DIM), f32), tiny(seq_count), tiny(cols), tiny(rows),
            pltpu.VMEM((8, HEAD_DIM), f32), tiny(2), pltpu.VMEM((8, HEAD_DIM), f32),
            pltpu.SMEM(norm_gains.shape, f32), pltpu.SMEM(tile_lists.T.shape, jnp.int32),
            dma((2,)),
            dma((3,)), dma((2, 3)), dma((2, chips // 2)), dma((2, chips // 2)), dma(()), dma((2,)), dma((2, 3)), dma((3,)), dma((7,)), dma((7,)),
        ],
        compiler_params=pltpu.CompilerParams(
            collective_id=0, has_side_effects=True, vmem_limit_bytes=32 * 1024 * 1024
        ),
    )(*(pltpu.with_memory_space_constraint(x, pltpu.HBM) for x in fixed), clip_lengths)
    return pl.pallas_call(
        deliver,
        out_shape=(shaped, shaped, shaped, jax.ShapeDtypeStruct(norm_gains.shape, f32)),
        in_specs=[vmem] * 4,
        out_specs=(hbm,) * 4,
        scratch_shapes=[pltpu.VMEM(norm_gains.shape, f32), dma((4,))],
        compiler_params=pltpu.CompilerParams(vmem_limit_bytes=4 * 1024 * 1024),
    )(dq, dk, dv, gain_sum)


def solution(mesh):
    placed = (
        P("dp", "seq", None),
        P("dp", "seq", None),
        P("dp", "seq", None),
        P("dp", "seq", None),
        P(None, "dp"),
        P(),
        P("dp"),
    )
    return jax.shard_map(
        body,
        mesh=mesh,
        in_specs=placed,
        out_specs=(P("dp", "seq", None), P("dp", "seq", None), P("dp", "seq", None), P(None, "dp")),
        check_vma=False,
    )
```

```python
import functools
import math


import jax
import jax.numpy as jnp
from jax import lax
from jax.experimental import pallas as pl
from jax.experimental.pallas import tpu as pltpu
import ml_dtypes
from jax.sharding import PartitionSpec as P

HEAD_DIM = 128
TILE = 64
EPS = 1e-06
BLOCK = 256
MESH = pl.DeviceIdType.MESH
FACTOR = 1.0 / math.sqrt(HEAD_DIM)
BLOCKED = -30000.0
TWICE = math.log(2.0) / FACTOR


def wait_bytes(ref, sem):
    pltpu.make_async_copy(ref, ref, sem).wait()


def wait_many(ref, count, sem):
    if count:
        wait_bytes(ref.at[pl.ds(0, count)], sem)


def total_of(ref):
    total = ref[0]
    for i in range(1, ref.shape[0]):
        total = total + ref[i]
    return total


def rms_inverse(wide):
    return lax.rsqrt(jnp.mean(wide * wide, axis=-1, keepdims=True) + EPS)


def rms_back(wide, inverse, gain_row, upstream):
    scaled = upstream * gain_row
    inner = jnp.mean(wide * scaled, axis=-1, keepdims=True)
    grad = inverse * scaled - wide * (inverse * inverse * inverse * inner)
    return grad.astype(jnp.bfloat16), jnp.sum(upstream * wide * inverse, axis=0, keepdims=True)


def kernel(
    sizes,
    q_in, k_in, v_in, c_in, g_hbm, lists_hbm, lengths,
    dq_out, dk_out, dv_out, gain_out,
    xq, xk, xv, cot, oq, ok, ov,
    qa, ka, kt, live, wbuf, gbuf, dk_acc, dv_acc,
    gsrc, gx, gy, ysrc, gains, gacc, hz, hx, hy, hsrc, hsrc2, hsum,
    g_raw, lists, tsem, ahead, behind,
    fsend, frecv, csend, crecv, osem, psem, rsend, orecv, gsend, grecv,
):
    chips, shard, per_chip, cols, rows = sizes
    seq = lax.axis_index("seq")
    dp = lax.axis_index("dp")
    chip, core = seq // 2, seq % 2
    row, col = dp // cols, dp % cols
    total = 2 * chips * shard
    blocks = total // BLOCK

    small = ((g_hbm, g_raw), (lists_hbm, lists))
    for index, (source, landing) in enumerate(small):
        pltpu.make_async_copy(source, landing, tsem.at[index]).start()

    barrier = pltpu.get_barrier_semaphore()

    after = 2 * ((chip + 1) % chips) + core
    before = 2 * ((chip + chips - 1) % chips) + core
    partner = 2 * chip + 1 - core

    def tell(sem, target):
        pl.semaphore_signal(sem, inc=1, device_id={"seq": target}, device_id_type=MESH)

    def greet_col(i, carry):
        pl.semaphore_signal(barrier, inc=1, device_id={"dp": row * cols + (col + i) % cols}, device_id_type=MESH)
        return carry

    def greet_row(i, carry):
        pl.semaphore_signal(barrier, inc=1, device_id={"dp": (row + i) % rows * cols + col}, device_id_type=MESH)
        return carry

    for target in (after, before, partner):
        tell(barrier, target)

    hub = 1
    is_hub = seq == hub

    @pl.when(is_hub)
    def _():
        lax.fori_loop(1, cols, greet_col, 0)
        lax.fori_loop(1, rows, greet_row, 0)

    @pl.when(is_hub)
    def _():
        pl.semaphore_wait(barrier, 3 + cols - 1 + rows - 1)

    @pl.when(seq != hub)
    def _():
        pl.semaphore_wait(barrier, 3)

    def send_gx(i, carry):
        pltpu.make_async_remote_copy(
            src_ref=gsrc, dst_ref=gx.at[col], send_sem=gsend.at[0], recv_sem=grecv.at[0],
            device_id={"dp": row * cols + (col + i) % cols}, device_id_type=MESH,
        ).start()
        return carry

    def send_gy(i, carry):
        pltpu.make_async_remote_copy(
            src_ref=ysrc, dst_ref=gy.at[row], send_sem=gsend.at[1], recv_sem=grecv.at[1],
            device_id={"dp": (row + i) % rows * cols + col}, device_id_type=MESH,
        ).start()
        return carry

    def send_gains(i, carry):
        pltpu.make_async_remote_copy(
            src_ref=gains, dst_ref=gains, send_sem=gsend.at[5], recv_sem=grecv.at[5],
            device_id={"seq": (seq + i) % (2 * chips)}, device_id_type=MESH,
        ).start()
        return carry

    arrays = ((q_in, xq), (k_in, xk), (v_in, xv))
    my_rows = pl.ds(pl.multiple_of(seq * shard, shard), shard)

    def near(i):
        half = i // 2 + 1
        return (chip + half * (1 - 2 * (i % 2)) + chips) % chips

    def pass_on(origin, step, way, side):
        source = c_in.at[0] if step == 1 else cot.at[origin, core]
        pltpu.make_async_remote_copy(
            src_ref=source, dst_ref=cot.at[origin, core],
            send_sem=csend.at[side, step - 1], recv_sem=crecv.at[side, step - 1],
            device_id={"seq": 2 * ((chip + way + chips) % chips) + core}, device_id_type=MESH,
        ).start()

    def passed(step, side, sems):
        wait_bytes(cot.at[0, 0], sems.at[side, step - 1])

    own_cot = pltpu.make_async_copy(c_in.at[0], cot.at[chip, core], osem)
    own_cot.start()
    last_step = chips // 2

    def spread_head(which):
        owner, slot = which % 2, which // 2

        def to_chip(target, start_kind):
            lanes = pl.ds(pl.multiple_of((target * per_chip + which) * HEAD_DIM, HEAD_DIM), HEAD_DIM)
            for index, (source, landing) in enumerate(arrays):
                src = source.at[0, :, lanes]
                dst = landing.at[slot, my_rows, :]
                if start_kind == "local":
                    pltpu.make_async_copy(src, dst, frecv.at[slot, index]).start()
                else:
                    pltpu.make_async_remote_copy(
                        src_ref=src, dst_ref=dst, send_sem=fsend.at[index], recv_sem=frecv.at[slot, index],
                        device_id={"seq": 2 * target + owner}, device_id_type=MESH,
                    ).start()

        def remote(i, carry):
            to_chip(near(i), "remote")
            return carry

        def at_home():
            @pl.when(core == owner)
            def _():
                to_chip(chip, "local")

            @pl.when(core != owner)
            def _():
                to_chip(chip, "remote")

        return remote, at_home

    def level(n):
        if n > 1:
            pl.semaphore_wait(ahead.at[n - 2], 1)
            if n <= last_step:
                pl.semaphore_wait(behind.at[n - 2], 1)
        if n <= last_step:
            tell(ahead.at[n - 1], before)
        if n < last_step:
            tell(behind.at[n - 1], after)

    level(1)
    remote, at_home = spread_head(0)
    for step in range(1, last_step):
        if step == 1:
            pass_on(chip, 1, 1, 0)
            pass_on(chip, 1, -1, 1)
        level(step + 1)
        if step > 1:
            for side, way in ((0, 1), (1, -1)):
                passed(step - 1, side, crecv)
                pass_on((chip - (step - 1) * way + chips) % chips, step, way, side)
        remote(2 * step - 2, 0)
        remote(2 * step - 1, 0)
    level(last_step + 1)
    for side in range(2):
        passed(last_step - 1, side, crecv)
    way = 1 - 2 * core
    pass_on((chip - (last_step - 1) * way + chips) % chips, last_step, way, 0)
    remote(chips - 2, 0)
    at_home()
    for index, (source, landing) in enumerate(small):
        pltpu.make_async_copy(source, landing, tsem.at[index]).wait()

    lane = lax.broadcasted_iota(jnp.int32, (8, HEAD_DIM), 1)
    sub = lax.broadcasted_iota(jnp.int32, (8, HEAD_DIM), 0)
    owned = g_raw.shape[1]
    spread = jnp.zeros((8, HEAD_DIM), jnp.float32)
    for r in range(2):
        for c in range(owned):
            spot = jnp.logical_and(sub == r, lane == dp * owned + c)
            spread = jnp.where(spot, g_raw[r, c], spread)
    gsrc[...] = spread

    lanes = lax.broadcasted_iota(jnp.int32, (TILE, HEAD_DIM), 1)
    places = lax.broadcasted_iota(jnp.int32, (TILE, HEAD_DIM), 0)
    length = lengths[0]
    high = float(ml_dtypes.bfloat16(TWICE))
    low = float(ml_dtypes.bfloat16(TWICE - high))

    def mask_tile(t, carry):
        named = jnp.zeros((TILE, HEAD_DIM), jnp.int32)
        for n in range(lists.shape[0]):
            named = named + (lanes % 32 == lists[n, t]).astype(jnp.int32)
        first = jnp.where(named > 0, jnp.where(named > 1, high, 0.0), BLOCKED)
        second = jnp.where(named > 1, low, 0.0)
        bias = jnp.where(lanes < 32, first, jnp.where(lanes < 64, second, 0.0))
        bias = jnp.where(lanes == 64, BLOCKED, bias)
        here = pl.ds(pl.multiple_of(t * TILE, TILE), TILE)
        qa[here, HEAD_DIM:] = bias.astype(jnp.bfloat16)
        mark = jnp.logical_and(lanes % 32 == t, lanes < 64)
        past = jnp.logical_and(lanes == 64, t * TILE + places >= length)
        ka[here, HEAD_DIM:] = jnp.where(jnp.logical_or(mark, past), 1.0, 0.0).astype(jnp.bfloat16)
        return carry

    tiles = total // TILE
    lax.fori_loop(0, tiles // 4, mask_tile, 0)

    @pl.when(is_hub)
    def _():
        lax.fori_loop(1, cols, send_gx, 0)
        gx[col] = gsrc[...]

    lax.fori_loop(tiles // 4, tiles // 2, mask_tile, 0)

    @pl.when(is_hub)
    def _():
        wait_many(gx, cols - 1, grecv.at[0])
        ysrc[...] = total_of(gx)

    lax.fori_loop(tiles // 2, 3 * tiles // 4, mask_tile, 0)

    @pl.when(is_hub)
    def _():
        lax.fori_loop(1, rows, send_gy, 0)
        gy[row] = ysrc[...]
        wait_many(gy, rows - 1, grecv.at[1])
        gains[...] = total_of(gy)

    lax.fori_loop(3 * tiles // 4, tiles, mask_tile, 0)
    gacc[...] = jnp.zeros_like(gacc)

    @pl.when(is_hub)
    def _():
        lax.fori_loop(1, 2 * chips, send_gains, 0)

    for which in range(1, per_chip):
        remote, at_home = spread_head(which)
        lax.fori_loop(0, chips - 1, remote, 0)
        at_home()

    passed(last_step, 0, crecv)
    own_cot.wait()
    forward = pltpu.make_async_remote_copy(
        src_ref=cot.at[:, core], dst_ref=cot.at[:, core], send_sem=psem.at[0], recv_sem=psem.at[1],
        device_id={"seq": partner}, device_id_type=MESH,
    )
    forward.start()
    forward.wait()

    @pl.when(seq != hub)
    def _():
        wait_bytes(gains, grecv.at[5])


    def live_block(i, carry):
        tokens = i * BLOCK + lax.broadcasted_iota(jnp.int32, (BLOCK, HEAD_DIM), 0)
        block = cot[i].reshape(BLOCK, HEAD_DIM).astype(jnp.float32)
        here = pl.ds(pl.multiple_of(i * BLOCK, BLOCK), BLOCK)
        live[here, :] = jnp.where(tokens < length, block, 0.0).astype(jnp.bfloat16)
        return carry

    lax.fori_loop(0, blocks, live_block, 0)
    gain_q, gain_k = gains[0:1, :], gains[1:2, :]

    def one_head(slot, carry):
        for index, (_, landing) in enumerate(arrays):
            wait_bytes(landing.at[slot], frecv.at[slot, index])

        def block_rows(i):
            return pl.ds(pl.multiple_of(i * BLOCK, BLOCK), BLOCK)

        def prepare(i, carry):
            here = block_rows(i)
            wide = xk[slot, here, :].astype(jnp.float32)
            norm = (wide * rms_inverse(wide) * gain_k).astype(jnp.bfloat16)
            ka[here, :HEAD_DIM] = norm
            kt[:, here] = norm.T
            wide = xq[slot, here, :].astype(jnp.float32)
            qa[here, :HEAD_DIM] = (wide * rms_inverse(wide) * gain_q).astype(jnp.bfloat16)
            zero = jnp.zeros((BLOCK, HEAD_DIM), jnp.float32)
            dk_acc[here, :] = zero
            dv_acc[here, :] = zero
            return carry

        lax.fori_loop(0, blocks, prepare, 0, unroll=2)

        nt = (((1,), (1,)), ((), ()))

        def query_block(b, carry):
            here = block_rows(b)
            q_block = qa[here, :]
            q_norm = q_block[:, :HEAD_DIM]
            live_rows = live[here, :]

            def scores(i, sums):
                den, mixed = sums
                keys = block_rows(i)
                logits = lax.dot_general(ka[keys, :], q_block, nt, preferred_element_type=jnp.float32)
                weight = jnp.exp(logits * FACTOR)
                grad = lax.dot_general(xv[slot, keys, :], live_rows, nt, preferred_element_type=jnp.float32)
                wbuf[keys, :] = weight
                gbuf[keys, :] = grad
                den = den + jnp.sum(weight, axis=0, keepdims=True)
                mixed = mixed + jnp.sum(weight * grad, axis=0, keepdims=True)
                return den, mixed

            zero = jnp.zeros((1, BLOCK), jnp.float32)
            den, mixed = lax.fori_loop(0, blocks, scores, (zero, zero), unroll=True)
            inv = 1.0 / den
            diag = mixed * inv

            def grads(i, dq_t):
                keys = block_rows(i)
                prob = wbuf[keys, :] * inv
                prob_low = prob.astype(jnp.bfloat16)
                grad_score = (prob * (gbuf[keys, :] - diag)).astype(jnp.bfloat16)
                dv_acc[keys, :] += jnp.dot(prob_low, live_rows, preferred_element_type=jnp.float32)
                dk_acc[keys, :] += jnp.dot(grad_score, q_norm, preferred_element_type=jnp.float32)
                return dq_t + jnp.dot(kt[:, keys], grad_score, preferred_element_type=jnp.float32)

            dq_t = lax.fori_loop(
                0, blocks, grads, jnp.zeros((HEAD_DIM, BLOCK), jnp.float32), unroll=True
            )
            upstream = (dq_t.T * FACTOR).astype(jnp.bfloat16).astype(jnp.float32)
            wide = xq[slot, here, :].astype(jnp.float32)
            grad, gain = rms_back(wide, rms_inverse(wide), gain_q, upstream)
            oq[slot, here, :] = grad
            gacc[0:1, :] += gain
            return carry

        lax.fori_loop(0, blocks, query_block, 0)

        def finish(i, carry):
            here = block_rows(i)
            upstream = (dk_acc[here, :] * FACTOR).astype(jnp.bfloat16).astype(jnp.float32)
            wide = xk[slot, here, :].astype(jnp.float32)
            grad, gain = rms_back(wide, rms_inverse(wide), gain_k, upstream)
            ok[slot, here, :] = grad
            ov[slot, here, :] = dv_acc[here, :].astype(jnp.bfloat16)
            gacc[1:2, :] += gain
            return carry

        lax.fori_loop(0, blocks, finish, 0, unroll=2)

        @pl.when(slot == 1 - core)
        def _():
            hsrc[...] = gacc[...]
            hz[seq] = gacc[...]

        head = chip * per_chip + core + 2 * slot
        out_lanes = pl.ds(pl.multiple_of(head * HEAD_DIM, HEAD_DIM), HEAD_DIM)
        results = ((oq, dq_out), (ok, dk_out), (ov, dv_out))

        def give_back(target, core_to, local):
            other = 2 * target + core_to
            rows = pl.ds(pl.multiple_of(other * shard, shard), shard)
            for index, (source, landing) in enumerate(results):
                src = source.at[slot, rows, :]
                dst = landing.at[0, :, out_lanes]
                if local:
                    pltpu.make_async_copy(src, dst, orecv.at[index]).start()
                else:
                    pltpu.make_async_remote_copy(
                        src_ref=src, dst_ref=dst, send_sem=rsend.at[slot, index], recv_sem=orecv.at[index],
                        device_id={"seq": other}, device_id_type=MESH,
                    ).start()

        def back(i, carry):
            give_back(near(i), core, False)
            give_back(near(i), 1 - core, False)
            return carry

        lax.fori_loop(0, 2, back, 0)

        @pl.when(jnp.logical_and(slot == 1 - core, seq != hub))
        def _():
            pltpu.make_async_remote_copy(
                src_ref=hsrc, dst_ref=hz.at[seq], send_sem=gsend.at[2], recv_sem=grecv.at[2],
                device_id={"seq": hub}, device_id_type=MESH,
            ).start()

        lax.fori_loop(2, chips - 1, back, 0)
        give_back(chip, 1 - core, False)
        give_back(chip, core, True)
        return carry

    lax.fori_loop(0, 2 - core, one_head, 0)

    def send_hx(i, carry):
        pltpu.make_async_remote_copy(
            src_ref=hsrc2.at[0], dst_ref=hx.at[col], send_sem=gsend.at[3], recv_sem=grecv.at[3],
            device_id={"dp": row * cols + (col + i) % cols}, device_id_type=MESH,
        ).start()
        return carry

    def send_hy(i, carry):
        pltpu.make_async_remote_copy(
            src_ref=hsrc2.at[1], dst_ref=hy.at[row], send_sem=gsend.at[4], recv_sem=grecv.at[4],
            device_id={"dp": (row + i) % rows * cols + col}, device_id_type=MESH,
        ).start()
        return carry

    def send_total(i, carry):
        pltpu.make_async_remote_copy(
            src_ref=hsum, dst_ref=hsum, send_sem=gsend.at[6], recv_sem=grecv.at[6],
            device_id={"seq": (seq + i) % (2 * chips)}, device_id_type=MESH,
        ).start()
        return carry

    @pl.when(is_hub)
    def _():
        wait_many(hz, 2 * chips - 1, grecv.at[2])
        summed = total_of(hz)
        hsrc2[0] = summed
        hx[col] = summed
        lax.fori_loop(1, cols, send_hx, 0)
        wait_many(hx, cols - 1, grecv.at[3])
        summed = total_of(hx)
        hsrc2[1] = summed
        hy[row] = summed
        lax.fori_loop(1, rows, send_hy, 0)
        wait_many(hy, rows - 1, grecv.at[4])
        hsum[...] = total_of(hy)
        lax.fori_loop(1, 2 * chips, send_total, 0)
        wait_many(gx, cols - 1, gsend.at[0])
        wait_many(gy, rows - 1, gsend.at[1])
        wait_many(hx, cols - 1, gsend.at[3])
        wait_many(hy, rows - 1, gsend.at[4])
        wait_many(hz, 2 * chips - 1, gsend.at[5])
        wait_many(hz, 2 * chips - 1, gsend.at[6])

    @pl.when(seq != hub)
    def _():
        wait_bytes(hsrc, gsend.at[2])
        wait_bytes(hsum, grecv.at[6])

    gain_out[...] = hsum[...]

    for step in range(1, last_step):
        passed(step, 0, csend)
        passed(step, 1, csend)
    passed(last_step, 0, csend)
    count = chips * per_chip
    for index, (source, _) in enumerate(arrays):
        @pl.when(core == 0)
        def _():
            wait_bytes(source.at[0, :, pl.ds(0, (count - 2) * HEAD_DIM)], fsend.at[index])

        @pl.when(core == 1)
        def _():
            wait_bytes(source.at[0, :, pl.ds(0, (count - 1) * HEAD_DIM)], fsend.at[index])

    def sent(slot, carry):
        for index, buffer in enumerate((oq, ok, ov)):
            wait_bytes(buffer.at[slot, pl.ds(0, total - shard), :], rsend.at[slot, index])
        return carry

    lax.fori_loop(0, 2 - core, sent, 0)
    for index, out in enumerate((dq_out, dk_out, dv_out)):
        wait_bytes(out, orecv.at[index])


def deliver(q_ref, k_ref, v_ref, gain_ref, q_out, k_out, v_out, gain_hbm, gain_out, sems):
    copies = [
        pltpu.make_async_copy(source, out, sems.at[index])
        for index, (source, out) in enumerate(((q_ref, q_out), (k_ref, k_out), (v_ref, v_out)))
    ]
    for copy in copies:
        copy.start()
    owned = gain_out.shape[1]
    turned = pltpu.roll(gain_ref[...], HEAD_DIM - lax.axis_index("dp") * owned, 1)
    count = lax.axis_size("dp") * lax.axis_size("seq") * q_ref.shape[1] * (q_ref.shape[2] // HEAD_DIM)
    gain_out[...] = turned[:2, :owned] * (1.0 / math.sqrt(count))
    copies.append(pltpu.make_async_copy(gain_out, gain_hbm, sems.at[3]))
    copies[3].start()
    for copy in copies:
        copy.wait()


def body(queries, key_states, value_states, cotangent, norm_gains, tile_lists, clip_lengths):
    seq_count = lax.axis_size("seq")
    dp_count = lax.axis_size("dp")
    dp = lax.axis_index("dp")
    shard, width = queries.shape[1], queries.shape[2]
    heads = width // HEAD_DIM
    chips = seq_count // 2
    per_chip = heads // chips
    total = shard * seq_count
    owned = norm_gains.shape[1]
    cols = math.gcd(dp_count, 4)
    rows = dp_count // cols
    bf, f32 = jnp.bfloat16, jnp.float32
    hbm = pl.BlockSpec(memory_space=pltpu.HBM)
    vmem = pl.BlockSpec(memory_space=pltpu.VMEM)
    dma = pltpu.SemaphoreType.DMA
    shaped = jax.ShapeDtypeStruct(queries.shape, bf)
    pair = pltpu.VMEM((2, total, HEAD_DIM), bf)
    tiny = lambda n: pltpu.VMEM((n, 8, HEAD_DIM), f32)
    fixed = (queries, key_states, value_states, cotangent, norm_gains, tile_lists.T)
    dq, dk, dv, gain_sum = pl.pallas_call(
        functools.partial(kernel, (chips, shard, per_chip, cols, rows)),
        out_shape=(shaped, shaped, shaped, jax.ShapeDtypeStruct((8, HEAD_DIM), f32)),
        in_specs=[hbm] * 6 + [pl.BlockSpec(memory_space=pltpu.SMEM)],
        out_specs=(vmem, vmem, vmem, vmem),
        scratch_shapes=[
            pair, pair, pair, pltpu.VMEM((chips, 2, shard, HEAD_DIM), bf), pair, pair, pair,
            pltpu.VMEM((total, 2 * HEAD_DIM), bf), pltpu.VMEM((total, 2 * HEAD_DIM), bf),
            pltpu.VMEM((HEAD_DIM, total), bf), pltpu.VMEM((total, HEAD_DIM), bf),
            pltpu.VMEM((total, BLOCK), f32), pltpu.VMEM((total, BLOCK), f32),
            pltpu.VMEM((total, HEAD_DIM), f32), pltpu.VMEM((total, HEAD_DIM), f32),
            pltpu.VMEM((8, HEAD_DIM), f32), tiny(cols), tiny(rows), pltpu.VMEM((8, HEAD_DIM), f32),
            pltpu.VMEM((8, HEAD_DIM), f32),
            pltpu.VMEM((8, HEAD_DIM), f32), tiny(seq_count), tiny(cols), tiny(rows),
            pltpu.VMEM((8, HEAD_DIM), f32), tiny(2), pltpu.VMEM((8, HEAD_DIM), f32),
            pltpu.SMEM(norm_gains.shape, f32), pltpu.SMEM(tile_lists.T.shape, jnp.int32),
            dma((2,)), pltpu.SemaphoreType.REGULAR((chips // 2,)), pltpu.SemaphoreType.REGULAR((chips // 2 - 1,)),
            dma((3,)), dma((2, 3)), dma((2, chips // 2)), dma((2, chips // 2)), dma(()), dma((2,)), dma((2, 3)), dma((3,)), dma((7,)), dma((7,)),
        ],
        compiler_params=pltpu.CompilerParams(
            collective_id=0, has_side_effects=True, vmem_limit_bytes=32 * 1024 * 1024
        ),
    )(*(pltpu.with_memory_space_constraint(x, pltpu.HBM) for x in fixed), clip_lengths)
    return pl.pallas_call(
        deliver,
        out_shape=(shaped, shaped, shaped, jax.ShapeDtypeStruct(norm_gains.shape, f32)),
        in_specs=[vmem] * 4,
        out_specs=(hbm,) * 4,
        scratch_shapes=[pltpu.VMEM(norm_gains.shape, f32), dma((4,))],
        compiler_params=pltpu.CompilerParams(vmem_limit_bytes=4 * 1024 * 1024),
    )(dq, dk, dv, gain_sum)


def solution(mesh):
    placed = (
        P("dp", "seq", None),
        P("dp", "seq", None),
        P("dp", "seq", None),
        P("dp", "seq", None),
        P(None, "dp"),
        P(),
        P("dp"),
    )
    return jax.shard_map(
        body,
        mesh=mesh,
        in_specs=placed,
        out_specs=(P("dp", "seq", None), P("dp", "seq", None), P("dp", "seq", None), P(None, "dp")),
        check_vma=False,
    )
```

```python
import functools
import math


import jax
import jax.numpy as jnp
from jax import lax
from jax.experimental import pallas as pl
from jax.experimental.pallas import tpu as pltpu
import ml_dtypes
from jax.sharding import PartitionSpec as P

HEAD_DIM = 128
TILE = 64
EPS = 1e-06
BLOCK = 256
MESH = pl.DeviceIdType.MESH
FACTOR = 1.0 / math.sqrt(HEAD_DIM)
BLOCKED = -30000.0
TWICE = math.log(2.0) / FACTOR


def wait_bytes(ref, sem):
    pltpu.make_async_copy(ref, ref, sem).wait()


def wait_many(ref, count, sem):
    if count:
        wait_bytes(ref.at[pl.ds(0, count)], sem)


def total_of(ref):
    total = ref[0]
    for i in range(1, ref.shape[0]):
        total = total + ref[i]
    return total


def rms_inverse(wide):
    return lax.rsqrt(jnp.mean(wide * wide, axis=-1, keepdims=True) + EPS)


def rms_back(wide, inverse, gain_row, upstream):
    scaled = upstream * gain_row
    inner = jnp.mean(wide * scaled, axis=-1, keepdims=True)
    grad = inverse * scaled - wide * (inverse * inverse * inverse * inner)
    return grad.astype(jnp.bfloat16), jnp.sum(upstream * wide * inverse, axis=0, keepdims=True)


def kernel(
    sizes,
    q_in, k_in, v_in, c_in, g_hbm, lists_hbm, lengths,
    dq_out, dk_out, dv_out, gain_out,
    xq, xk, xv, cot, oq, ok, ov,
    qa, ka, kt, live, wbuf, gbuf, dk_acc, dv_acc,
    gsrc, gx, gy, ysrc, gains, gacc, hz, hx, hy, hsrc, hsrc2, hsum,
    g_raw, lists, tsem, ahead, behind,
    fsend, frecv, csend, crecv, osem, psem, rsend, orecv, gsend, grecv,
):
    chips, shard, per_chip, cols, rows = sizes
    seq = lax.axis_index("seq")
    dp = lax.axis_index("dp")
    chip, core = seq // 2, seq % 2
    row, col = dp // cols, dp % cols
    total = 2 * chips * shard
    blocks = total // BLOCK

    small = ((g_hbm, g_raw), (lists_hbm, lists))
    for index, (source, landing) in enumerate(small):
        pltpu.make_async_copy(source, landing, tsem.at[index]).start()

    barrier = pltpu.get_barrier_semaphore()

    after = 2 * ((chip + 1) % chips) + core
    before = 2 * ((chip + chips - 1) % chips) + core
    partner = 2 * chip + 1 - core

    def tell(sem, target):
        pl.semaphore_signal(sem, inc=1, device_id={"seq": target}, device_id_type=MESH)

    def greet_col(i, carry):
        pl.semaphore_signal(barrier, inc=1, device_id={"dp": row * cols + (col + i) % cols}, device_id_type=MESH)
        return carry

    def greet_row(i, carry):
        pl.semaphore_signal(barrier, inc=1, device_id={"dp": (row + i) % rows * cols + col}, device_id_type=MESH)
        return carry

    for target in (after, before, partner):
        tell(barrier, target)

    hub = 1
    is_hub = seq == hub

    @pl.when(is_hub)
    def _():
        lax.fori_loop(1, cols, greet_col, 0)
        lax.fori_loop(1, rows, greet_row, 0)

    @pl.when(is_hub)
    def _():
        pl.semaphore_wait(barrier, 3 + cols - 1 + rows - 1)

    @pl.when(seq != hub)
    def _():
        pl.semaphore_wait(barrier, 3)

    def send_gx(i, carry):
        pltpu.make_async_remote_copy(
            src_ref=gsrc, dst_ref=gx.at[col], send_sem=gsend.at[0], recv_sem=grecv.at[0],
            device_id={"dp": row * cols + (col + i) % cols}, device_id_type=MESH,
        ).start()
        return carry

    def send_gy(i, carry):
        pltpu.make_async_remote_copy(
            src_ref=ysrc, dst_ref=gy.at[row], send_sem=gsend.at[1], recv_sem=grecv.at[1],
            device_id={"dp": (row + i) % rows * cols + col}, device_id_type=MESH,
        ).start()
        return carry

    def send_gains(i, carry):
        pltpu.make_async_remote_copy(
            src_ref=gains, dst_ref=gains, send_sem=gsend.at[5], recv_sem=grecv.at[5],
            device_id={"seq": (seq + i) % (2 * chips)}, device_id_type=MESH,
        ).start()
        return carry

    arrays = ((q_in, xq), (k_in, xk), (v_in, xv))
    my_rows = pl.ds(pl.multiple_of(seq * shard, shard), shard)

    def near(i):
        half = i // 2 + 1
        return (chip + half * (1 - 2 * (i % 2)) + chips) % chips

    def pass_on(origin, step, way, side):
        source = c_in.at[0] if step == 1 else cot.at[origin, core]
        pltpu.make_async_remote_copy(
            src_ref=source, dst_ref=cot.at[origin, core],
            send_sem=csend.at[side, step - 1], recv_sem=crecv.at[side, step - 1],
            device_id={"seq": 2 * ((chip + way + chips) % chips) + core}, device_id_type=MESH,
        ).start()

    def passed(step, side, sems):
        wait_bytes(cot.at[0, 0], sems.at[side, step - 1])

    own_cot = pltpu.make_async_copy(c_in.at[0], cot.at[chip, core], osem)
    own_cot.start()
    last_step = chips // 2

    def spread_head(which):
        owner, slot = which % 2, which // 2

        def to_chip(target, start_kind):
            lanes = pl.ds(pl.multiple_of((target * per_chip + which) * HEAD_DIM, HEAD_DIM), HEAD_DIM)
            for index, (source, landing) in enumerate(arrays):
                src = source.at[0, :, lanes]
                dst = landing.at[slot, my_rows, :]
                if start_kind == "local":
                    pltpu.make_async_copy(src, dst, frecv.at[slot, index]).start()
                else:
                    pltpu.make_async_remote_copy(
                        src_ref=src, dst_ref=dst, send_sem=fsend.at[index], recv_sem=frecv.at[slot, index],
                        device_id={"seq": 2 * target + owner}, device_id_type=MESH,
                    ).start()

        def remote(i, carry):
            to_chip(near(i), "remote")
            return carry

        def at_home():
            @pl.when(core == owner)
            def _():
                to_chip(chip, "local")

            @pl.when(core != owner)
            def _():
                to_chip(chip, "remote")

        return remote, at_home

    def level(n):
        if n > 1:
            pl.semaphore_wait(ahead.at[n - 2], 1)
            if n <= last_step:
                pl.semaphore_wait(behind.at[n - 2], 1)
        if n <= last_step:
            tell(ahead.at[n - 1], before)
        if n < last_step:
            tell(behind.at[n - 1], after)

    level(1)
    remote, at_home = spread_head(0)
    for step in range(1, last_step):
        if step == 1:
            pass_on(chip, 1, 1, 0)
            pass_on(chip, 1, -1, 1)
        @pl.when(core == 0)
        def _():
            remote(2 * step - 2, 0)
            remote(2 * step - 1, 0)

        level(step + 1)
        if step > 1:
            for side, way in ((0, 1), (1, -1)):
                passed(step - 1, side, crecv)
                pass_on((chip - (step - 1) * way + chips) % chips, step, way, side)

        @pl.when(core == 1)
        def _():
            remote(2 * step - 2, 0)
            remote(2 * step - 1, 0)

    @pl.when(core == 0)
    def _():
        remote(chips - 2, 0)

    level(last_step + 1)
    for side in range(2):
        passed(last_step - 1, side, crecv)
    way = 1 - 2 * core
    pass_on((chip - (last_step - 1) * way + chips) % chips, last_step, way, 0)

    @pl.when(core == 1)
    def _():
        remote(chips - 2, 0)

    at_home()
    for index, (source, landing) in enumerate(small):
        pltpu.make_async_copy(source, landing, tsem.at[index]).wait()

    lane = lax.broadcasted_iota(jnp.int32, (8, HEAD_DIM), 1)
    sub = lax.broadcasted_iota(jnp.int32, (8, HEAD_DIM), 0)
    owned = g_raw.shape[1]
    spread = jnp.zeros((8, HEAD_DIM), jnp.float32)
    for r in range(2):
        for c in range(owned):
            spot = jnp.logical_and(sub == r, lane == dp * owned + c)
            spread = jnp.where(spot, g_raw[r, c], spread)
    gsrc[...] = spread

    lanes = lax.broadcasted_iota(jnp.int32, (TILE, HEAD_DIM), 1)
    places = lax.broadcasted_iota(jnp.int32, (TILE, HEAD_DIM), 0)
    length = lengths[0]
    high = float(ml_dtypes.bfloat16(TWICE))
    low = float(ml_dtypes.bfloat16(TWICE - high))

    def mask_tile(t, carry):
        named = jnp.zeros((TILE, HEAD_DIM), jnp.int32)
        for n in range(lists.shape[0]):
            named = named + (lanes % 32 == lists[n, t]).astype(jnp.int32)
        first = jnp.where(named > 0, jnp.where(named > 1, high, 0.0), BLOCKED)
        second = jnp.where(named > 1, low, 0.0)
        bias = jnp.where(lanes < 32, first, jnp.where(lanes < 64, second, 0.0))
        bias = jnp.where(lanes == 64, BLOCKED, bias)
        here = pl.ds(pl.multiple_of(t * TILE, TILE), TILE)
        qa[here, HEAD_DIM:] = bias.astype(jnp.bfloat16)
        mark = jnp.logical_and(lanes % 32 == t, lanes < 64)
        past = jnp.logical_and(lanes == 64, t * TILE + places >= length)
        ka[here, HEAD_DIM:] = jnp.where(jnp.logical_or(mark, past), 1.0, 0.0).astype(jnp.bfloat16)
        return carry

    tiles = total // TILE
    lax.fori_loop(0, tiles // 4, mask_tile, 0)

    @pl.when(is_hub)
    def _():
        lax.fori_loop(1, cols, send_gx, 0)
        gx[col] = gsrc[...]

    lax.fori_loop(tiles // 4, tiles // 2, mask_tile, 0)

    @pl.when(is_hub)
    def _():
        wait_many(gx, cols - 1, grecv.at[0])
        ysrc[...] = total_of(gx)

    lax.fori_loop(tiles // 2, 3 * tiles // 4, mask_tile, 0)

    @pl.when(is_hub)
    def _():
        lax.fori_loop(1, rows, send_gy, 0)
        gy[row] = ysrc[...]
        wait_many(gy, rows - 1, grecv.at[1])
        gains[...] = total_of(gy)

    lax.fori_loop(3 * tiles // 4, tiles, mask_tile, 0)
    gacc[...] = jnp.zeros_like(gacc)

    @pl.when(is_hub)
    def _():
        lax.fori_loop(1, 2 * chips, send_gains, 0)

    for which in range(1, per_chip):
        remote, at_home = spread_head(which)
        lax.fori_loop(0, chips - 1, remote, 0)
        at_home()

    passed(last_step, 0, crecv)
    own_cot.wait()
    forward = pltpu.make_async_remote_copy(
        src_ref=cot.at[:, core], dst_ref=cot.at[:, core], send_sem=psem.at[0], recv_sem=psem.at[1],
        device_id={"seq": partner}, device_id_type=MESH,
    )
    forward.start()
    forward.wait()

    @pl.when(seq != hub)
    def _():
        wait_bytes(gains, grecv.at[5])


    def live_block(i, carry):
        tokens = i * BLOCK + lax.broadcasted_iota(jnp.int32, (BLOCK, HEAD_DIM), 0)
        block = cot[i].reshape(BLOCK, HEAD_DIM).astype(jnp.float32)
        here = pl.ds(pl.multiple_of(i * BLOCK, BLOCK), BLOCK)
        live[here, :] = jnp.where(tokens < length, block, 0.0).astype(jnp.bfloat16)
        return carry

    lax.fori_loop(0, blocks, live_block, 0)
    gain_q, gain_k = gains[0:1, :], gains[1:2, :]

    def one_head(slot, carry):
        for index, (_, landing) in enumerate(arrays):
            wait_bytes(landing.at[slot], frecv.at[slot, index])

        def block_rows(i):
            return pl.ds(pl.multiple_of(i * BLOCK, BLOCK), BLOCK)

        def prepare(i, carry):
            here = block_rows(i)
            wide = xk[slot, here, :].astype(jnp.float32)
            norm = (wide * rms_inverse(wide) * gain_k).astype(jnp.bfloat16)
            ka[here, :HEAD_DIM] = norm
            kt[:, here] = norm.T
            wide = xq[slot, here, :].astype(jnp.float32)
            qa[here, :HEAD_DIM] = (wide * rms_inverse(wide) * gain_q).astype(jnp.bfloat16)
            zero = jnp.zeros((BLOCK, HEAD_DIM), jnp.float32)
            dk_acc[here, :] = zero
            dv_acc[here, :] = zero
            return carry

        lax.fori_loop(0, blocks, prepare, 0, unroll=2)

        nt = (((1,), (1,)), ((), ()))

        def query_block(b, carry):
            here = block_rows(b)
            q_block = qa[here, :]
            q_norm = q_block[:, :HEAD_DIM]
            live_rows = live[here, :]

            def scores(i, sums):
                den, mixed = sums
                keys = block_rows(i)
                logits = lax.dot_general(ka[keys, :], q_block, nt, preferred_element_type=jnp.float32)
                weight = jnp.exp(logits * FACTOR)
                grad = lax.dot_general(xv[slot, keys, :], live_rows, nt, preferred_element_type=jnp.float32)
                wbuf[keys, :] = weight
                gbuf[keys, :] = grad
                den = den + jnp.sum(weight, axis=0, keepdims=True)
                mixed = mixed + jnp.sum(weight * grad, axis=0, keepdims=True)
                return den, mixed

            zero = jnp.zeros((1, BLOCK), jnp.float32)
            den, mixed = lax.fori_loop(0, blocks, scores, (zero, zero), unroll=True)
            inv = 1.0 / den
            diag = mixed * inv

            def grads(i, dq_t):
                keys = block_rows(i)
                prob = wbuf[keys, :] * inv
                prob_low = prob.astype(jnp.bfloat16)
                grad_score = (prob * (gbuf[keys, :] - diag)).astype(jnp.bfloat16)
                dv_acc[keys, :] += jnp.dot(prob_low, live_rows, preferred_element_type=jnp.float32)
                dk_acc[keys, :] += jnp.dot(grad_score, q_norm, preferred_element_type=jnp.float32)
                return dq_t + jnp.dot(kt[:, keys], grad_score, preferred_element_type=jnp.float32)

            dq_t = lax.fori_loop(
                0, blocks, grads, jnp.zeros((HEAD_DIM, BLOCK), jnp.float32), unroll=True
            )
            upstream = (dq_t.T * FACTOR).astype(jnp.bfloat16).astype(jnp.float32)
            wide = xq[slot, here, :].astype(jnp.float32)
            grad, gain = rms_back(wide, rms_inverse(wide), gain_q, upstream)
            oq[slot, here, :] = grad
            gacc[0:1, :] += gain
            return carry

        lax.fori_loop(0, blocks, query_block, 0)

        def finish(i, carry):
            here = block_rows(i)
            upstream = (dk_acc[here, :] * FACTOR).astype(jnp.bfloat16).astype(jnp.float32)
            wide = xk[slot, here, :].astype(jnp.float32)
            grad, gain = rms_back(wide, rms_inverse(wide), gain_k, upstream)
            ok[slot, here, :] = grad
            ov[slot, here, :] = dv_acc[here, :].astype(jnp.bfloat16)
            gacc[1:2, :] += gain
            return carry

        lax.fori_loop(0, blocks, finish, 0, unroll=2)

        @pl.when(slot == 1 - core)
        def _():
            hsrc[...] = gacc[...]
            hz[seq] = gacc[...]

        head = chip * per_chip + core + 2 * slot
        out_lanes = pl.ds(pl.multiple_of(head * HEAD_DIM, HEAD_DIM), HEAD_DIM)
        results = ((oq, dq_out), (ok, dk_out), (ov, dv_out))

        def give_back(target, core_to, local):
            other = 2 * target + core_to
            rows = pl.ds(pl.multiple_of(other * shard, shard), shard)
            for index, (source, landing) in enumerate(results):
                src = source.at[slot, rows, :]
                dst = landing.at[0, :, out_lanes]
                if local:
                    pltpu.make_async_copy(src, dst, orecv.at[index]).start()
                else:
                    pltpu.make_async_remote_copy(
                        src_ref=src, dst_ref=dst, send_sem=rsend.at[slot, index], recv_sem=orecv.at[index],
                        device_id={"seq": other}, device_id_type=MESH,
                    ).start()

        def back(i, carry):
            give_back(near(i), core, False)
            give_back(near(i), 1 - core, False)
            return carry

        lax.fori_loop(0, 2, back, 0)

        @pl.when(jnp.logical_and(slot == 1 - core, seq != hub))
        def _():
            pltpu.make_async_remote_copy(
                src_ref=hsrc, dst_ref=hz.at[seq], send_sem=gsend.at[2], recv_sem=grecv.at[2],
                device_id={"seq": hub}, device_id_type=MESH,
            ).start()

        lax.fori_loop(2, chips - 1, back, 0)
        give_back(chip, 1 - core, False)
        give_back(chip, core, True)
        return carry

    lax.fori_loop(0, 2 - core, one_head, 0)

    def send_hx(i, carry):
        pltpu.make_async_remote_copy(
            src_ref=hsrc2.at[0], dst_ref=hx.at[col], send_sem=gsend.at[3], recv_sem=grecv.at[3],
            device_id={"dp": row * cols + (col + i) % cols}, device_id_type=MESH,
        ).start()
        return carry

    def send_hy(i, carry):
        pltpu.make_async_remote_copy(
            src_ref=hsrc2.at[1], dst_ref=hy.at[row], send_sem=gsend.at[4], recv_sem=grecv.at[4],
            device_id={"dp": (row + i) % rows * cols + col}, device_id_type=MESH,
        ).start()
        return carry

    def send_total(i, carry):
        pltpu.make_async_remote_copy(
            src_ref=hsum, dst_ref=hsum, send_sem=gsend.at[6], recv_sem=grecv.at[6],
            device_id={"seq": (seq + i) % (2 * chips)}, device_id_type=MESH,
        ).start()
        return carry

    @pl.when(is_hub)
    def _():
        wait_many(hz, 2 * chips - 1, grecv.at[2])
        summed = total_of(hz)
        hsrc2[0] = summed
        hx[col] = summed
        lax.fori_loop(1, cols, send_hx, 0)
        wait_many(hx, cols - 1, grecv.at[3])
        summed = total_of(hx)
        hsrc2[1] = summed
        hy[row] = summed
        lax.fori_loop(1, rows, send_hy, 0)
        wait_many(hy, rows - 1, grecv.at[4])
        hsum[...] = total_of(hy)
        lax.fori_loop(1, 2 * chips, send_total, 0)
        wait_many(gx, cols - 1, gsend.at[0])
        wait_many(gy, rows - 1, gsend.at[1])
        wait_many(hx, cols - 1, gsend.at[3])
        wait_many(hy, rows - 1, gsend.at[4])
        wait_many(hz, 2 * chips - 1, gsend.at[5])
        wait_many(hz, 2 * chips - 1, gsend.at[6])

    @pl.when(seq != hub)
    def _():
        wait_bytes(hsrc, gsend.at[2])
        wait_bytes(hsum, grecv.at[6])

    gain_out[...] = hsum[...]

    for step in range(1, last_step):
        passed(step, 0, csend)
        passed(step, 1, csend)
    passed(last_step, 0, csend)
    count = chips * per_chip
    for index, (source, _) in enumerate(arrays):
        @pl.when(core == 0)
        def _():
            wait_bytes(source.at[0, :, pl.ds(0, (count - 2) * HEAD_DIM)], fsend.at[index])

        @pl.when(core == 1)
        def _():
            wait_bytes(source.at[0, :, pl.ds(0, (count - 1) * HEAD_DIM)], fsend.at[index])

    def sent(slot, carry):
        for index, buffer in enumerate((oq, ok, ov)):
            wait_bytes(buffer.at[slot, pl.ds(0, total - shard), :], rsend.at[slot, index])
        return carry

    lax.fori_loop(0, 2 - core, sent, 0)
    for index, out in enumerate((dq_out, dk_out, dv_out)):
        wait_bytes(out, orecv.at[index])


def deliver(q_ref, k_ref, v_ref, gain_ref, q_out, k_out, v_out, gain_hbm, gain_out, sems):
    copies = [
        pltpu.make_async_copy(source, out, sems.at[index])
        for index, (source, out) in enumerate(((q_ref, q_out), (k_ref, k_out), (v_ref, v_out)))
    ]
    for copy in copies:
        copy.start()
    owned = gain_out.shape[1]
    turned = pltpu.roll(gain_ref[...], HEAD_DIM - lax.axis_index("dp") * owned, 1)
    count = lax.axis_size("dp") * lax.axis_size("seq") * q_ref.shape[1] * (q_ref.shape[2] // HEAD_DIM)
    gain_out[...] = turned[:2, :owned] * (1.0 / math.sqrt(count))
    copies.append(pltpu.make_async_copy(gain_out, gain_hbm, sems.at[3]))
    copies[3].start()
    for copy in copies:
        copy.wait()


def body(queries, key_states, value_states, cotangent, norm_gains, tile_lists, clip_lengths):
    seq_count = lax.axis_size("seq")
    dp_count = lax.axis_size("dp")
    dp = lax.axis_index("dp")
    shard, width = queries.shape[1], queries.shape[2]
    heads = width // HEAD_DIM
    chips = seq_count // 2
    per_chip = heads // chips
    total = shard * seq_count
    owned = norm_gains.shape[1]
    cols = math.gcd(dp_count, 4)
    rows = dp_count // cols
    bf, f32 = jnp.bfloat16, jnp.float32
    hbm = pl.BlockSpec(memory_space=pltpu.HBM)
    vmem = pl.BlockSpec(memory_space=pltpu.VMEM)
    dma = pltpu.SemaphoreType.DMA
    shaped = jax.ShapeDtypeStruct(queries.shape, bf)
    pair = pltpu.VMEM((2, total, HEAD_DIM), bf)
    tiny = lambda n: pltpu.VMEM((n, 8, HEAD_DIM), f32)
    fixed = (queries, key_states, value_states, cotangent, norm_gains, tile_lists.T)
    dq, dk, dv, gain_sum = pl.pallas_call(
        functools.partial(kernel, (chips, shard, per_chip, cols, rows)),
        out_shape=(shaped, shaped, shaped, jax.ShapeDtypeStruct((8, HEAD_DIM), f32)),
        in_specs=[hbm] * 6 + [pl.BlockSpec(memory_space=pltpu.SMEM)],
        out_specs=(vmem, vmem, vmem, vmem),
        scratch_shapes=[
            pair, pair, pair, pltpu.VMEM((chips, 2, shard, HEAD_DIM), bf), pair, pair, pair,
            pltpu.VMEM((total, 2 * HEAD_DIM), bf), pltpu.VMEM((total, 2 * HEAD_DIM), bf),
            pltpu.VMEM((HEAD_DIM, total), bf), pltpu.VMEM((total, HEAD_DIM), bf),
            pltpu.VMEM((total, BLOCK), f32), pltpu.VMEM((total, BLOCK), f32),
            pltpu.VMEM((total, HEAD_DIM), f32), pltpu.VMEM((total, HEAD_DIM), f32),
            pltpu.VMEM((8, HEAD_DIM), f32), tiny(cols), tiny(rows), pltpu.VMEM((8, HEAD_DIM), f32),
            pltpu.VMEM((8, HEAD_DIM), f32),
            pltpu.VMEM((8, HEAD_DIM), f32), tiny(seq_count), tiny(cols), tiny(rows),
            pltpu.VMEM((8, HEAD_DIM), f32), tiny(2), pltpu.VMEM((8, HEAD_DIM), f32),
            pltpu.SMEM(norm_gains.shape, f32), pltpu.SMEM(tile_lists.T.shape, jnp.int32),
            dma((2,)), pltpu.SemaphoreType.REGULAR((chips // 2,)), pltpu.SemaphoreType.REGULAR((chips // 2 - 1,)),
            dma((3,)), dma((2, 3)), dma((2, chips // 2)), dma((2, chips // 2)), dma(()), dma((2,)), dma((2, 3)), dma((3,)), dma((7,)), dma((7,)),
        ],
        compiler_params=pltpu.CompilerParams(
            collective_id=0, has_side_effects=True, vmem_limit_bytes=32 * 1024 * 1024
        ),
    )(*(pltpu.with_memory_space_constraint(x, pltpu.HBM) for x in fixed), clip_lengths)
    return pl.pallas_call(
        deliver,
        out_shape=(shaped, shaped, shaped, jax.ShapeDtypeStruct(norm_gains.shape, f32)),
        in_specs=[vmem] * 4,
        out_specs=(hbm,) * 4,
        scratch_shapes=[pltpu.VMEM(norm_gains.shape, f32), dma((4,))],
        compiler_params=pltpu.CompilerParams(vmem_limit_bytes=4 * 1024 * 1024),
    )(dq, dk, dv, gain_sum)


def solution(mesh):
    placed = (
        P("dp", "seq", None),
        P("dp", "seq", None),
        P("dp", "seq", None),
        P("dp", "seq", None),
        P(None, "dp"),
        P(),
        P("dp"),
    )
    return jax.shard_map(
        body,
        mesh=mesh,
        in_specs=placed,
        out_specs=(P("dp", "seq", None), P("dp", "seq", None), P("dp", "seq", None), P(None, "dp")),
        check_vma=False,
    )
```
